32 devices in a mesh: gx: 4 (over x, core), gy: 8 (over z, y).
Axes of the slice: x: 2, y: 2, z: 4, core: 2. Of those that a mesh axis runs over, the one named last changes fastest.
Arguments:
- tokens: bfloat16 [4096, 2048], P('gy', 'gx'), may hold values from -6 to 6
- attn_gain: bfloat16 [2048], P('gy'), may hold values from 0.099609375 to 1.8984375
- attn_shift: bfloat16 [2048], P('gy'), may hold values from -3 to 3
- ffn_gain: bfloat16 [2048], P('gy'), may hold values from 0.099609375 to 1.8984375
- ffn_shift: bfloat16 [2048], P('gy'), may hold values from -3 to 3
- qkv_weight: bfloat16 [2048, 6144], P('gy', 'gx'), may hold values from -1 to 1
- qkv_bias: bfloat16 [6144], P(('gx', 'gy')), may hold values from -3 to 3
- out_weight: bfloat16 [2048, 2048], P('gx', 'gy'), may hold values from -6 to 6
- out_bias: bfloat16 [2048], P(('gx', 'gy')), may hold values from -3 to 3
- up_weight: bfloat16 [2048, 8192], P('gy', 'gx'), may hold values from -0.125 to 0.125
- up_bias: bfloat16 [8192], P(('gx', 'gy')), may hold values from -3 to 3
- down_weight: bfloat16 [8192, 2048], P('gx', 'gy'), may hold values from -0.0625 to 0.0625
- down_bias: bfloat16 [2048], P(('gx', 'gy')), may hold values from -3 to 3
- cotangent: bfloat16 [4096, 2048], P('gy', 'gx'), may hold values from -6 to 6
Outputs:
- output: bfloat16 [4096, 2048], P('gy', 'gx')
- grad_tokens: float32 [4096, 2048], P('gy', 'gx')
- grad_attn_gain: float32 [2048], P('gy')
- grad_attn_shift: float32 [2048], P('gy')
- grad_ffn_gain: float32 [2048], P('gy')
- grad_ffn_shift: float32 [2048], P('gy')
- grad_qkv_weight: float32 [2048, 6144], P('gy', 'gx')
- grad_qkv_bias: float32 [6144], P(('gx', 'gy'))
- grad_out_weight: float32 [2048, 2048], P('gx', 'gy')
- grad_out_bias: float32 [2048], P(('gx', 'gy'))
- grad_up_weight: float32 [2048, 8192], P('gy', 'gx')
- grad_up_bias: float32 [8192], P(('gx', 'gy'))
- grad_down_weight: float32 [8192, 2048], P('gx', 'gy')
- grad_down_bias: float32 [2048], P(('gx', 'gy'))
The draws below stay inside these ranges and needn't reach their ends.
All inputs are finite; a program needn't handle non-finite values.
Results may differ from the reference program's by a relative error of at most 0.025.
Values may be sent and summed in bfloat16 or wider, within the bound.
A program may use at most 192 MiB of HBM per device.

```python
import math
import jax
import jax.numpy as jnp
from jax import lax

D = 2048
HEADS = 8
HEAD = 256
ROT = 64
FF = 8192
TOK_DEV = 512
SPAN = 8
SEQ_LEN = 4096
SEQS = 1
TOTAL = 4096


def draw_qkv_weight(key, part):
    base = jnp.clip(jax.random.normal(key, (D, HEADS, 3, HEAD), jnp.float32), -6.0, 6.0) * D ** (-0.5)
    return base.reshape(D, 3 * D).astype(jnp.bfloat16)


def shard_levels(stream_key, extent, split, least, largest):
    def one(dim, parts):
        steps = jax.random.uniform(jax.random.fold_in(jax.random.fold_in(stream_key, 6), dim), (parts,), jnp.float32, least / len(split), largest / len(split))
        return jnp.repeat(jnp.exp(steps), extent[dim] // parts).reshape((-1,) + (1,) * (len(extent) - dim - 1))

    level = one(*split[0])
    for cut in split[1:]:
        level = level * one(*cut)
    return level


def gaussian(rng, shape, scale, bound, cuts=(), kind=jnp.bfloat16):
    level = shard_levels(rng, shape, cuts, -0.22, 0.18) if cuts else 1.0
    result = jax.random.normal(rng, shape, jnp.float32) * scale * level
    return jnp.minimum(jnp.maximum(result, -bound), bound).astype(kind)


def setup_inputs(seed: int = 0) -> dict:
    arg_keys = jax.random.split(jax.random.key(seed), 15)
    return {
        "tokens": gaussian(arg_keys[0], (TOTAL, D), 1.0, 6.0, ((0, 8), (1, 4))),
        "attn_gain": jnp.clip(1.0 + 0.18 * jax.random.normal(arg_keys[1], (D,), jnp.float32), 0.099609375, 1.8984375).astype(jnp.bfloat16),
        "attn_shift": gaussian(arg_keys[2], (D,), 0.3, 3.0, ((0, 8),)),
        "ffn_gain": jnp.clip(1.0 + 0.18 * jax.random.normal(arg_keys[3], (D,), jnp.float32), 0.099609375, 1.8984375).astype(jnp.bfloat16),
        "ffn_shift": gaussian(arg_keys[4], (D,), 0.3, 3.0, ((0, 8),)),
        "qkv_weight": draw_qkv_weight(jax.random.fold_in(arg_keys[14], 71), 0),
        "qkv_bias": gaussian(arg_keys[6], (3 * D,), 0.5, 3.0, ((0, 32),)),
        "out_weight": gaussian(arg_keys[7], (D, D), (max(2 * D // (TOK_DEV * SPAN), 1)) ** -0.5, 6.0, ((0, 4), (1, 8))),
        "out_bias": gaussian(arg_keys[8], (D,), 0.5, 3.0, ((0, 32),)),
        "up_weight": gaussian(arg_keys[9], (D, FF), D ** -0.5, 0.125, ((0, 8), (1, 4))),
        "up_bias": gaussian(arg_keys[10], (FF,), 0.5, 3.0, ((0, 32),)),
        "down_weight": gaussian(arg_keys[11], (FF, D), FF ** -0.5, 0.0625, ((0, 4), (1, 8))),
        "down_bias": gaussian(arg_keys[12], (D,), 0.5, 3.0, ((0, 32),)),
        "cotangent": gaussian(arg_keys[13], (TOTAL, D), 1.0, 6.0, ((0, 8), (1, 4))),
    }


@jax.custom_vjp
def low(v):
    return lax.optimization_barrier(v.astype(jnp.bfloat16)).astype(jnp.float32)

@jax.custom_vjp
def low_back(v):
    return v

def low_keep(v):
    return (low(v), None)

def low_pass(kept, grad):
    return (grad,)

def back_keep(v):
    return (v, None)

def back_low(kept, grad):
    return (low(grad),)
low.defvjp(low_keep, low_pass)
low_back.defvjp(back_keep, back_low)

def norm_rows(values, gain, shift):
    average = lax.optimization_barrier(jnp.mean(values, axis=-1, keepdims=True))
    centred = values - average
    spread = lax.optimization_barrier(jnp.mean(centred * centred, axis=-1, keepdims=True))
    return centred * lax.rsqrt(spread + 1e-05) * gain + shift

def rotary_angles(positions):
    half_rot = ROT // 2
    frequency = 10000.0 ** (-(2.0 * jnp.arange(half_rot).astype(jnp.float32)) / ROT)
    return positions.astype(jnp.float32)[:, None] * frequency[None, :]

def rotate(heads, angles):
    half_rot = angles.shape[-1]
    cosine = jnp.cos(angles)[:, None, :]
    sine = jnp.sin(angles)[:, None, :]
    first = heads[..., :half_rot]
    second = heads[..., half_rot:2 * half_rot]
    return jnp.concatenate([first * cosine - second * sine, second * cosine + first * sine, heads[..., 2 * half_rot:]], axis=-1)

def attend(queries, keys, values):
    length = queries.shape[0]
    block_rows = math.gcd(length, 512)
    factor = HEAD ** (-0.5)
    key_pos = jnp.arange(length, dtype=jnp.int32)
    highest = lax.Precision.HIGHEST

    def one_block(number):
        offset = number * block_rows
        block_q = lax.dynamic_slice_in_dim(queries, offset, block_rows, 0)
        scores = jnp.einsum('qhd,khd->hqk', block_q, keys, precision=highest) * factor
        query_pos = offset + jnp.arange(block_rows, dtype=jnp.int32)
        visible = key_pos[None, :] <= query_pos[:, None]
        scores = low_back(jnp.where(visible[None], scores, -1e+30))
        row_max = lax.optimization_barrier(jnp.max(scores, axis=-1, keepdims=True))
        log_total = row_max + jnp.log(lax.optimization_barrier(jnp.sum(jnp.exp(scores - row_max), axis=-1, keepdims=True)))
        probs = low(jnp.exp(scores - log_total))
        return jnp.einsum('hqk,khd->qhd', probs, values, precision=highest)
    blocks = lax.map(jax.checkpoint(one_block), jnp.arange(length // block_rows, dtype=jnp.int32))
    return blocks.reshape(length, HEADS, HEAD)

def attend_sequence(triple):
    return attend(triple[0], triple[1], triple[2])

def layer(tokens, attn_gain, attn_shift, ffn_gain, ffn_shift, qkv_weight, qkv_bias, out_weight, out_bias, up_weight, up_bias, down_weight, down_bias):
    length = tokens.shape[0]
    highest = lax.Precision.HIGHEST
    normed_attn = low(norm_rows(tokens, attn_gain, attn_shift))
    normed_ffn = low(norm_rows(tokens, ffn_gain, ffn_shift))
    mixed = low_back(jnp.dot(normed_attn, qkv_weight, precision=highest) + qkv_bias)
    mixed = mixed.reshape(length, HEADS, 3, HEAD)
    angles = rotary_angles(jnp.arange(length, dtype=jnp.int32) % SEQ_LEN)
    queries = low(rotate(mixed[:, :, 0], angles))
    keys = low(rotate(mixed[:, :, 1], angles))
    values = low(mixed[:, :, 2])
    shape_seq = (SEQS, SEQ_LEN, HEADS, HEAD)
    attended = lax.map(attend_sequence, (queries.reshape(shape_seq), keys.reshape(shape_seq), values.reshape(shape_seq)))
    context = low(low_back(attended.reshape(length, HEADS, HEAD))).reshape(length, D)
    hidden_pre = low_back(jnp.dot(normed_ffn, up_weight, precision=highest) + up_bias)
    hidden = low(jax.nn.gelu(hidden_pre, approximate=False))
    branch = jnp.dot(context, out_weight, precision=highest) + jnp.dot(hidden, down_weight, precision=highest)
    return tokens + branch + out_bias + down_bias

def reference(tokens, attn_gain, attn_shift, ffn_gain, ffn_shift, qkv_weight, qkv_bias, out_weight, out_bias, up_weight, up_bias, down_weight, down_bias, cotangent):
    output, pullback = jax.vjp(layer, tokens.astype(jnp.float32), attn_gain.astype(jnp.float32), attn_shift.astype(jnp.float32), ffn_gain.astype(jnp.float32), ffn_shift.astype(jnp.float32), qkv_weight.astype(jnp.float32), qkv_bias.astype(jnp.float32), out_weight.astype(jnp.float32), out_bias.astype(jnp.float32), up_weight.astype(jnp.float32), up_bias.astype(jnp.float32), down_weight.astype(jnp.float32), down_bias.astype(jnp.float32))
    grads = pullback(cotangent.astype(jnp.float32))
    return (output.astype(jnp.bfloat16), grads[0], grads[1], grads[2], grads[3], grads[4], grads[5], grads[6], grads[7], grads[8], grads[9], grads[10], grads[11], grads[12])
```

```python
import functools

import jax
import jax.numpy as jnp
from jax import lax
from jax.experimental import pallas as pl
from jax.experimental.pallas import tpu as pltpu
from jax.sharding import PartitionSpec as P

HEAD = 256
ROT = 64
SPAN = 8


eps_norm = 1e-05


def passed_along(value, axis, steps):
    count = lax.axis_size(axis)
    leading, last = (max(0, -steps), min(count, count - steps))
    return lax.ppermute(value, axis, [(source, source + steps) for source in range(leading, last)])


def norm_rows(values, gain, shift):
    average = jnp.mean(values, axis=-1, keepdims=True)
    centred = values - average
    spread = jnp.mean(centred * centred, axis=-1, keepdims=True)
    return centred * lax.rsqrt(spread + eps_norm) * gain + shift


def exact_gelu(values):
    return jax.nn.gelu(values, approximate=False)


def angle_table(positions):
    half_rot = ROT // 2
    frequency = 10000.0 ** (-(2.0 * jnp.arange(half_rot).astype(jnp.float32)) / ROT)
    return positions.astype(jnp.float32)[:, None] * frequency[None, :]


def rotate(heads, angles):
    half_rot = angles.shape[-1]
    cosine = jnp.cos(angles)[:, None, :]
    sine = jnp.sin(angles)[:, None, :]
    first = heads[..., :half_rot]
    second = heads[..., half_rot : 2 * half_rot]
    return jnp.concatenate(
        [
            first * cosine - second * sine,
            second * cosine + first * sine,
            heads[..., 2 * half_rot :],
        ],
        axis=-1,
    )


def unrotate(heads, angles):
    half_rot = angles.shape[-1]
    cosine = jnp.cos(angles)[:, None, :]
    sine = jnp.sin(angles)[:, None, :]
    first = heads[..., :half_rot]
    second = heads[..., half_rot : 2 * half_rot]
    return jnp.concatenate(
        [
            first * cosine + second * sine,
            second * cosine - first * sine,
            heads[..., 2 * half_rot :],
        ],
        axis=-1,
    )


def contract_last(left, right):
    return lax.dot_general(
        left, right, (((1,), (1,)), ((), ())), preferred_element_type=jnp.float32
    )


def contract_first(left, right):
    return lax.dot_general(
        left, right, (((0,), (0,)), ((), ())), preferred_element_type=jnp.float32
    )


def visible_mask(query_pos, key_pos, seq_len):
    return (
        (key_pos[None, :] <= query_pos[:, None])
        & (key_pos >= 0)[None, :]
        & (query_pos < seq_len)[:, None]
    )


def pair_grads(
    query_set, grad_set, log_total, delta, query_pos, key_set, value_set, key_pos, seq_len
):
    factor = HEAD ** (-0.5)
    scores = (
        jnp.einsum("qhd,khd->hqk", query_set, key_set, preferred_element_type=jnp.float32) * factor
    )
    visible = visible_mask(query_pos, key_pos, seq_len)
    probs = jnp.where(
        visible[None], jnp.exp(jnp.where(visible[None], scores - log_total[:, :, None], 0.0)), 0.0
    )
    grad_probs = jnp.einsum("qhd,khd->hqk", grad_set, value_set, preferred_element_type=jnp.float32)
    grad_scores = (probs * (grad_probs - delta[:, :, None])).astype(jnp.bfloat16)
    grad_q = (
        jnp.einsum("hqk,khd->qhd", grad_scores, key_set, preferred_element_type=jnp.float32)
        * factor
    )
    grad_k = (
        jnp.einsum("hqk,qhd->khd", grad_scores, query_set, preferred_element_type=jnp.float32)
        * factor
    )
    grad_v = jnp.einsum(
        "hqk,qhd->khd", probs.astype(jnp.bfloat16), grad_set, preferred_element_type=jnp.float32
    )
    return (grad_q, grad_k, grad_v)


def local(
    tokens,
    attn_gain,
    attn_shift,
    ffn_gain,
    ffn_shift,
    qkv_weight,
    qkv_bias,
    out_weight,
    out_bias,
    up_weight,
    up_bias,
    down_weight,
    down_bias,
    cotangent,
):
    tok_rows = tokens.shape[0]
    width_part = tokens.shape[1]
    local_heads = qkv_weight.shape[1] // (3 * HEAD)
    factor = HEAD ** (-0.5)
    seq_len = tok_rows * SPAN
    local_start = lax.axis_index("gy") % SPAN * tok_rows
    positions = local_start + jnp.arange(tok_rows, dtype=jnp.int32)
    angles = angle_table(positions)
    full_rows = lax.all_gather(tokens, "gx", axis=1, tiled=True).astype(jnp.float32)
    qkv_full, up_full, qkv_shift, up_shift, gain_attn, shift_attn, gain_ffn, shift_ffn = (
        lax.all_gather(qkv_weight, "gy", axis=0, tiled=True),
        lax.all_gather(up_weight, "gy", axis=0, tiled=True),
        lax.all_gather(qkv_bias, "gy", axis=0, tiled=True),
        lax.all_gather(up_bias, "gy", axis=0, tiled=True),
        lax.all_gather(attn_gain, "gy", axis=0, tiled=True),
        lax.all_gather(attn_shift, "gy", axis=0, tiled=True),
        lax.all_gather(ffn_gain, "gy", axis=0, tiled=True),
        lax.all_gather(ffn_shift, "gy", axis=0, tiled=True),
    )
    normed_attn, back_attn = jax.vjp(
        norm_rows, full_rows, gain_attn.astype(jnp.float32), shift_attn.astype(jnp.float32)
    )
    normed_ffn, back_ffn = jax.vjp(
        norm_rows, full_rows, gain_ffn.astype(jnp.float32), shift_ffn.astype(jnp.float32)
    )
    normed_attn = normed_attn.astype(jnp.bfloat16)
    normed_ffn = normed_ffn.astype(jnp.bfloat16)
    mixed = jnp.dot(normed_attn, qkv_full, preferred_element_type=jnp.float32) + qkv_shift.astype(
        jnp.float32
    )
    mixed = mixed.reshape(tok_rows, local_heads, 3, HEAD)
    queries = rotate(mixed[:, :, 0], angles).astype(jnp.bfloat16)
    keys = rotate(mixed[:, :, 1], angles).astype(jnp.bfloat16)
    values = mixed[:, :, 2].astype(jnp.bfloat16)
    head_cols = local_heads * HEAD

    def attend_piece(carried, piece_keys, piece_values, offset):
        row_max, row_total, summed = carried
        length = piece_keys.shape[0]
        scores = (
            jnp.einsum("qhd,khd->hqk", queries, piece_keys, preferred_element_type=jnp.float32)
            * factor
        )
        visible = visible_mask(positions, offset + jnp.arange(length, dtype=jnp.int32), seq_len)
        scores = jnp.where(visible[None], scores, -1e30)
        new_max = jnp.maximum(row_max, jnp.max(scores, axis=-1))
        weights = jnp.where(visible[None], jnp.exp(scores - new_max[:, :, None]), 0.0)
        shrink = jnp.exp(row_max - new_max)
        row_total = row_total * shrink + jnp.sum(weights, axis=-1)
        summed = summed * jnp.transpose(shrink)[:, :, None] + jnp.einsum(
            "hqk,khd->qhd",
            weights.astype(jnp.bfloat16),
            piece_values,
            preferred_element_type=jnp.float32,
        )
        return (new_max, row_total, summed)

    start_state = (
        jnp.full((local_heads, tok_rows), -1e30, jnp.float32),
        jnp.zeros((local_heads, tok_rows), jnp.float32),
        jnp.zeros((tok_rows, local_heads, HEAD), jnp.float32),
    )
    state = attend_piece(start_state, keys, values, local_start)
    kv_stack = jnp.stack(
        [keys.reshape(tok_rows, head_cols), values.reshape(tok_rows, head_cols)], axis=0
    )
    for step in range(1, SPAN):
        arrived = passed_along(kv_stack, "gy", step)
        state = attend_piece(
            state,
            arrived[0].reshape(tok_rows, local_heads, HEAD),
            arrived[1].reshape(tok_rows, local_heads, HEAD),
            local_start - step * tok_rows,
        )
    row_max, row_total, summed = state
    log_total = row_max + jnp.log(row_total)
    context_sum = summed / jnp.transpose(row_total)[:, :, None]
    context_low = context_sum.reshape(tok_rows, head_cols).astype(jnp.bfloat16)
    out_full, down_full, out_cols, down_cols = (
        lax.all_gather(out_weight, "gy", axis=1, tiled=True),
        lax.all_gather(down_weight, "gy", axis=1, tiled=True),
        lax.all_gather(out_bias, "gy", axis=0, tiled=True),
        lax.all_gather(down_bias, "gy", axis=0, tiled=True),
    )
    hidden_pre = jnp.dot(normed_ffn, up_full, preferred_element_type=jnp.float32) + up_shift.astype(
        jnp.float32
    )
    hidden, gelu_back = jax.vjp(exact_gelu, hidden_pre)
    hidden_low = hidden.astype(jnp.bfloat16)
    branch_sum = jnp.dot(context_low, out_full, preferred_element_type=jnp.float32) + jnp.dot(
        hidden_low, down_full, preferred_element_type=jnp.float32
    )
    mixed_out = lax.psum_scatter(
        branch_sum.astype(jnp.bfloat16), "gx", scatter_dimension=1, tiled=True
    ).astype(jnp.float32)
    output = (
        tokens.astype(jnp.float32)
        + mixed_out
        + out_cols.astype(jnp.float32)
        + down_cols.astype(jnp.float32)
    ).astype(jnp.bfloat16)
    grad_rows = lax.all_gather(cotangent, "gx", axis=1, tiled=True)
    grad_context = contract_last(grad_rows, out_full).astype(jnp.bfloat16)
    grad_hidden = contract_last(grad_rows, down_full)
    grad_pre = gelu_back(grad_hidden)[0].astype(jnp.bfloat16)
    grad_out_local = contract_first(context_low, grad_rows)
    grad_down_local = contract_first(hidden_low, grad_rows)
    grad_bias_cols = jnp.sum(cotangent.astype(jnp.float32), axis=0)
    grad_out_w, grad_down_w, grad_bias = (
        lax.psum_scatter(
            grad_out_local.astype(jnp.bfloat16), "gy", scatter_dimension=1, tiled=True
        ).astype(jnp.float32),
        lax.psum_scatter(
            grad_down_local.astype(jnp.bfloat16), "gy", scatter_dimension=1, tiled=True
        ).astype(jnp.float32),
        lax.psum_scatter(
            grad_bias_cols.astype(jnp.bfloat16), "gy", scatter_dimension=0, tiled=True
        ).astype(jnp.float32),
    )
    grad_heads = grad_context.reshape(tok_rows, local_heads, HEAD)
    delta = jnp.einsum("qhd,qhd->hq", grad_heads.astype(jnp.float32), context_sum)
    grad_q, grad_k, grad_v = pair_grads(
        queries, grad_heads, log_total, delta, positions, keys, values, positions, seq_len
    )
    row_stack = jnp.stack(
        [
            queries.reshape(tok_rows, head_cols),
            grad_context,
            keys.reshape(tok_rows, head_cols),
            values.reshape(tok_rows, head_cols),
        ],
        axis=0,
    )
    stat_stack = jnp.stack([log_total, delta], axis=0)
    for step in [item for item in range(1 - SPAN, SPAN) if item != 0]:
        arrived = passed_along(row_stack, "gy", step)
        stats = passed_along(stat_stack, "gy", step)
        piece_pos = local_start - step * tok_rows + jnp.arange(tok_rows, dtype=jnp.int32)
        other_q = arrived[0].reshape(tok_rows, local_heads, HEAD)
        other_g = arrived[1].reshape(tok_rows, local_heads, HEAD)
        other_k = arrived[2].reshape(tok_rows, local_heads, HEAD)
        other_v = arrived[3].reshape(tok_rows, local_heads, HEAD)
        if step > 0:
            part_q, unused_k, unused_v = pair_grads(
                queries,
                grad_heads,
                log_total,
                delta,
                positions,
                other_k,
                other_v,
                piece_pos,
                seq_len,
            )
            grad_q = grad_q + part_q
        else:
            unused_q, part_k, part_v = pair_grads(
                other_q, other_g, stats[0], stats[1], piece_pos, keys, values, positions, seq_len
            )
            grad_k = grad_k + part_k
            grad_v = grad_v + part_v
    grad_mixed = jnp.stack([unrotate(grad_q, angles), unrotate(grad_k, angles), grad_v], axis=2)
    grad_mixed = grad_mixed.reshape(tok_rows, 3 * head_cols).astype(jnp.bfloat16)
    grad_norm_attn = contract_last(grad_mixed, qkv_full)
    grad_norm_ffn = contract_last(grad_pre, up_full)
    sum_attn, sum_ffn = (
        lax.psum(grad_norm_attn.astype(jnp.bfloat16), "gx").astype(jnp.float32),
        lax.psum(grad_norm_ffn.astype(jnp.bfloat16), "gx").astype(jnp.float32),
    )
    input_attn, gain_grad_attn, shift_grad_attn = back_attn(sum_attn)
    input_ffn, gain_grad_ffn, shift_grad_ffn = back_ffn(sum_ffn)
    own_cols = lax.dynamic_slice_in_dim(
        input_attn + input_ffn, lax.axis_index("gx") * width_part, width_part, 1
    )
    grad_tokens = cotangent.astype(jnp.float32) + own_cols
    grad_qkv_local = contract_first(normed_attn, grad_mixed)
    grad_up_local = contract_first(normed_ffn, grad_pre)
    grad_qkv_cols = jnp.sum(grad_mixed.astype(jnp.float32), axis=0)
    grad_up_cols = jnp.sum(grad_pre.astype(jnp.float32), axis=0)
    (
        grad_qkv_w,
        grad_up_w,
        grad_qkv_b,
        grad_up_b,
        grad_gain_attn,
        grad_shift_attn,
        grad_gain_ffn,
        grad_shift_ffn,
    ) = (
        lax.psum_scatter(
            grad_qkv_local.astype(jnp.bfloat16), "gy", scatter_dimension=0, tiled=True
        ).astype(jnp.float32),
        lax.psum_scatter(
            grad_up_local.astype(jnp.bfloat16), "gy", scatter_dimension=0, tiled=True
        ).astype(jnp.float32),
        lax.psum_scatter(
            grad_qkv_cols.astype(jnp.bfloat16), "gy", scatter_dimension=0, tiled=True
        ).astype(jnp.float32),
        lax.psum_scatter(
            grad_up_cols.astype(jnp.bfloat16), "gy", scatter_dimension=0, tiled=True
        ).astype(jnp.float32),
        lax.psum_scatter(
            gain_grad_attn.astype(jnp.bfloat16), "gy", scatter_dimension=0, tiled=True
        ).astype(jnp.float32),
        lax.psum_scatter(
            shift_grad_attn.astype(jnp.bfloat16), "gy", scatter_dimension=0, tiled=True
        ).astype(jnp.float32),
        lax.psum_scatter(
            gain_grad_ffn.astype(jnp.bfloat16), "gy", scatter_dimension=0, tiled=True
        ).astype(jnp.float32),
        lax.psum_scatter(
            shift_grad_ffn.astype(jnp.bfloat16), "gy", scatter_dimension=0, tiled=True
        ).astype(jnp.float32),
    )
    return (
        output,
        grad_tokens,
        grad_gain_attn,
        grad_shift_attn,
        grad_gain_ffn,
        grad_shift_ffn,
        grad_qkv_w,
        grad_qkv_b,
        grad_out_w,
        grad_bias,
        grad_up_w,
        grad_up_b,
        grad_down_w,
        grad_bias,
    )


def swap(value, axis, mask):
    count = lax.axis_size(axis)
    return lax.ppermute(value, axis, [(source, source ^ mask) for source in range(count)])


def gather_gy(block):
    zs = [block] + [swap(block, "gy", 2 * step) for step in (1, 2, 3)]
    out = []
    for piece in zs:
        out += [piece, swap(piece, "gy", 1)]
    return out


def scatter_gy(groups, extra=None):
    count, rows, width = groups.shape
    pairs = groups.reshape(count // 2, 2, rows, width)
    mine = pairs[:, 0]
    away = swap(pairs[:, 1], "gy", 1)
    total = mine.astype(jnp.float32) + away.astype(jnp.float32)
    low = total.astype(jnp.bfloat16)
    result = total[0]
    for step in (1, 2, 3):
        result = result + swap(low[step], "gy", 2 * step).astype(jnp.float32)
    return result


def gather_gx(block):
    far = swap(block, "gx", 2)
    near = swap(block, "gx", 1)
    last = swap(far, "gx", 1)
    return [block, near, far, last]


def scatter_gx(parts):
    near = swap(jnp.stack([parts[1], parts[3]]), "gx", 1).astype(jnp.float32)
    keep = parts[0].astype(jnp.float32) + near[0]
    send = (parts[2].astype(jnp.float32) + near[1]).astype(jnp.bfloat16)
    return keep + swap(send, "gx", 2).astype(jnp.float32)


def chunk_mask(sub, where, tile, chunk, queries, keys):
    row = lax.broadcasted_iota(jnp.int32, (queries, keys), 0)
    col = lax.broadcasted_iota(jnp.int32, (queries, keys), 1)
    gx = where[0]
    gy = where[1]
    query_pos = 4 * sub * (2 * tile + ((row // sub) ^ (gy & 1))) + sub * gx + row % sub
    key_pos = 4 * sub * chunk + sub * ((col // sub) ^ gx) + col % sub
    return key_pos <= query_pos


def load_chunk(sub, refs, where, chunk, low, high):
    start = pl.multiple_of((chunk ^ where[1]) * sub, sub)
    return jnp.concatenate([ref[pl.ds(start, sub), low:high] for ref in refs], axis=0)


def attend_kernel(sub, where, q_ref, kv0, kv1, kv2, kv3, ctx_ref, low_ref, log_ref):
    tile = pl.program_id(0)
    refs = (kv0, kv1, kv2, kv3)
    query = q_ref[...]
    rows = query.shape[0]

    def step(chunk, carried, masked):
        top, total, summed = carried
        keys = load_chunk(sub, refs, where, chunk, 0, HEAD)
        values = load_chunk(sub, refs, where, chunk, HEAD, 2 * HEAD)
        scores = contract_last(query, keys)
        if masked:
            visible = chunk_mask(sub, where, tile, chunk, rows, 4 * sub)
            scores = jnp.where(visible, scores, -1e30)
        new_top = jnp.maximum(top, jnp.max(scores, axis=-1, keepdims=True))
        weights = jnp.exp(scores - new_top)
        if masked:
            weights = jnp.where(visible, weights, 0.0)
        shrink = jnp.exp(top - new_top)
        total = total * shrink + jnp.sum(weights, axis=-1, keepdims=True)
        summed = summed * shrink + jnp.dot(
            weights.astype(jnp.bfloat16), values, preferred_element_type=jnp.float32
        )
        return new_top, total, summed

    state = (
        jnp.full((rows, 1), -1e30, jnp.float32),
        jnp.zeros((rows, 1), jnp.float32),
        jnp.zeros((rows, HEAD), jnp.float32),
    )
    state = lax.fori_loop(0, 2 * tile, lambda c, s: step(c, s, False), state)
    state = step(2 * tile, state, True)
    state = step(2 * tile + 1, state, True)
    top, total, summed = state
    context = summed / total
    ctx_ref[...] = context
    low_ref[...] = context.astype(jnp.bfloat16)
    log_ref[...] = jnp.broadcast_to(top + jnp.log(total), log_ref.shape)


def attend(where, query, parts):
    rows = query.shape[0]
    sub = rows // SPAN
    tile = 2 * sub
    spec = pl.BlockSpec((tile, HEAD), lambda m, w: (m ^ (w[1] // 2), 0))
    full = pl.BlockSpec((rows, 2 * HEAD), lambda m, w: (0, 0))
    return pl.pallas_call(
        functools.partial(attend_kernel, sub),
        grid_spec=pltpu.PrefetchScalarGridSpec(
            num_scalar_prefetch=1,
            grid=(rows // tile,),
            in_specs=[spec] + [full] * 4,
            out_specs=[spec, spec, pl.BlockSpec((tile, 128), lambda m, w: (m ^ (w[1] // 2), 0))],
        ),
        out_shape=[
            jax.ShapeDtypeStruct((rows, HEAD), jnp.float32),
            jax.ShapeDtypeStruct((rows, HEAD), jnp.bfloat16),
            jax.ShapeDtypeStruct((rows, 128), jnp.float32),
        ],
        cost_estimate=pl.CostEstimate(
            flops=10 * rows * rows * HEAD, bytes_accessed=10 * rows * HEAD * 2, transcendentals=2 * rows * rows
        ),
        name="attend",
    )(where, query, *parts)


def attend_back_kernel(
    sub, where, q_ref, g_ref, ctx_ref, log_ref, kv0, kv1, kv2, kv3, dq_ref, d0, d1, d2, d3, acc
):
    tile = pl.program_id(0)
    refs = (kv0, kv1, kv2, kv3)
    query = q_ref[...]
    grad = g_ref[...]
    rows = query.shape[0]
    log_total = log_ref[:, 0:1]
    delta = jnp.sum(grad.astype(jnp.float32) * ctx_ref[...], axis=-1, keepdims=True)

    @pl.when(tile == 0)
    def _():
        acc[...] = jnp.zeros_like(acc)

    def step(chunk, dq, masked):
        keys = load_chunk(sub, refs, where, chunk, 0, HEAD)
        values = load_chunk(sub, refs, where, chunk, HEAD, 2 * HEAD)
        scores = contract_last(query, keys)
        probs = scores - log_total
        if masked:
            visible = chunk_mask(sub, where, tile, chunk, rows, 4 * sub)
            probs = jnp.where(visible, jnp.exp(jnp.where(visible, probs, 0.0)), 0.0)
        else:
            probs = jnp.exp(probs)
        grad_probs = contract_last(grad, values)
        grad_scores = (probs * (grad_probs - delta)).astype(jnp.bfloat16)
        acc[chunk, :, 0:HEAD] += contract_first(grad_scores, query)
        acc[chunk, :, HEAD : 2 * HEAD] += contract_first(probs.astype(jnp.bfloat16), grad)
        return dq + jnp.dot(grad_scores, keys, preferred_element_type=jnp.float32)

    dq = jnp.zeros((rows, HEAD), jnp.float32)
    dq = lax.fori_loop(0, 2 * tile, lambda c, s: step(c, s, False), dq)
    dq = step(2 * tile, dq, True)
    dq = step(2 * tile + 1, dq, True)
    dq_ref[...] = dq * HEAD ** (-0.5)

    @pl.when(tile == pl.num_programs(0) - 1)
    def _():
        def flush(chunk, carried):
            start = pl.multiple_of((chunk ^ where[1]) * sub, sub)
            for part, out in enumerate((d0, d1, d2, d3)):
                out[pl.ds(start, sub), :] = acc[chunk, part * sub : (part + 1) * sub, :].astype(
                    jnp.bfloat16
                )
            return carried

        lax.fori_loop(0, acc.shape[0], flush, 0)


def attend_back(where, query, grad, context, log_total, parts):
    rows = query.shape[0]
    sub = rows // SPAN
    tile = 2 * sub
    spec = pl.BlockSpec((tile, HEAD), lambda m, w: (m ^ (w[1] // 2), 0))
    full = pl.BlockSpec((rows, 2 * HEAD), lambda m, w: (0, 0))
    return pl.pallas_call(
        functools.partial(attend_back_kernel, sub),
        grid_spec=pltpu.PrefetchScalarGridSpec(
            num_scalar_prefetch=1,
            grid=(rows // tile,),
            in_specs=[spec, spec, spec, pl.BlockSpec((tile, 128), lambda m, w: (m ^ (w[1] // 2), 0))]
            + [full] * 4,
            out_specs=[spec] + [full] * 4,
            scratch_shapes=[pltpu.VMEM((rows // sub, 4 * sub, 2 * HEAD), jnp.float32)],
        ),
        out_shape=[jax.ShapeDtypeStruct((rows, HEAD), jnp.float32)]
        + [jax.ShapeDtypeStruct((rows, 2 * HEAD), jnp.bfloat16)] * 4,
        cost_estimate=pl.CostEstimate(
            flops=26 * rows * rows * HEAD, bytes_accessed=20 * rows * HEAD * 2, transcendentals=2 * rows * rows
        ),
        name="attend_back",
    )(where, query, grad, context, log_total, *parts)


def regroup(
    tokens,
    attn_gain,
    attn_shift,
    ffn_gain,
    ffn_shift,
    qkv_weight,
    qkv_bias,
    out_weight,
    out_bias,
    up_weight,
    up_bias,
    down_weight,
    down_bias,
    cotangent,
):
    f32, bf16 = jnp.float32, jnp.bfloat16
    gx, gy = lax.axis_index("gx"), lax.axis_index("gy")
    nx, ny = lax.axis_size("gx"), lax.axis_size("gy")
    where = jnp.stack([gx, gy]).astype(jnp.int32)
    block_rows, part = tokens.shape
    width = nx * part
    sub = block_rows // nx
    rows = sub * ny
    unit = up_weight.shape[1] // ny
    krows = qkv_weight.shape[0]
    head_cols = 3 * HEAD

    def line(*pieces):
        flat = jnp.concatenate(pieces)
        return jnp.pad(flat, (0, part - flat.shape[0]))[None]

    small = jnp.concatenate(
        [
            line(attn_gain, attn_shift),
            line(ffn_gain, ffn_shift),
            line(up_bias, qkv_bias),
            line(out_bias, down_bias),
            jnp.zeros((12, part), bf16),
        ]
    )
    sent = jnp.concatenate(
        [
            tokens.reshape(nx, sub, part),
            jnp.broadcast_to(small[None], (nx, 16, part)),
            cotangent.reshape(nx, sub, part),
        ],
        axis=1,
    )
    came = lax.all_to_all(sent, "gx", 0, 0, tiled=True)
    came = jnp.transpose(came, (1, 0, 2)).reshape(2 * sub + 16, width)
    own_rows = came[: sub + 16]
    own_cot = came[sub + 16 :]

    heads = qkv_weight.reshape(krows, 2, head_cols)
    outs = out_weight.reshape(2, HEAD, out_weight.shape[1])
    pack = [
        jnp.concatenate([heads[:, a], outs[a]], axis=1) for a in (0, 1)
    ]
    odd = (gy % 2) == 1
    send = [jnp.where(odd, pack[1 - s], pack[s]) for s in (0, 1)]
    pairs = [
        [((i * ny + j), ((j // 2) * ny + 2 * i + (j + s) % 2)) for i in range(nx) for j in range(ny)]
        for s in (0, 1)
    ]
    got = [lax.ppermute(send[s], ("gx", "gy"), pairs[s]) for s in (0, 1)]
    two = jnp.stack([jnp.where(odd, got[1], got[0]), jnp.where(odd, got[0], got[1])])

    gathered = gather_gy(own_rows)
    att_parts = gather_gx(two)

    att = jnp.zeros((nx,) + two.shape, bf16)
    for m in range(4):
        att = lax.dynamic_update_index_in_dim(att, att_parts[m], gx ^ m, 0)
    att = att.reshape(ny, krows, head_cols + krows)
    qkv_full = att[:, :, :head_cols].reshape(width, head_cols)
    out_full = jnp.transpose(att[:, :, head_cols:], (1, 0, 2)).reshape(HEAD, width)

    ffn = jnp.concatenate(
        [
            jnp.transpose(up_weight.reshape(krows, ny, unit), (1, 0, 2)),
            down_weight.reshape(ny, unit, down_weight.shape[1]),
        ],
        axis=1,
    )
    ffn = lax.all_to_all(ffn, "gy", 0, 0, tiled=True)
    ffn_parts = gather_gx(ffn)
    cots = gather_gy(own_cot)
    cot = jnp.stack(cots).reshape(rows, width)
    up_full = jnp.concatenate([p[:, :krows].reshape(width, unit) for p in ffn_parts], axis=1)
    down_full = jnp.concatenate(
        [jnp.transpose(p[:, krows:], (1, 0, 2)).reshape(unit, width) for p in ffn_parts], axis=0
    )

    lines = jnp.zeros((ny, 4, nx, part), bf16)
    for m in range(8):
        lines = lax.dynamic_update_index_in_dim(
            lines, gathered[m][sub : sub + 4].reshape(4, nx, part), gy ^ m, 0
        )
    lines = lines.astype(f32)
    quarter = krows
    gain_attn = lines[:, 0, 0, :quarter].reshape(1, width)
    shift_attn = lines[:, 0, 0, quarter:].reshape(1, width)
    gain_ffn = lines[:, 1, 0, :quarter].reshape(1, width)
    shift_ffn = lines[:, 1, 0, quarter:].reshape(1, width)
    up_rows = lax.dynamic_index_in_dim(lines[:, 2, :, :unit], gy, 0, keepdims=False)
    up_shift = jnp.concatenate(
        [lax.dynamic_index_in_dim(up_rows, gx ^ m, 0, keepdims=False) for m in range(4)]
    )
    bias_size = qkv_bias.shape[0]
    qkv_all = jnp.transpose(lines[:, 2, :, unit : unit + bias_size], (1, 0, 2)).reshape(
        ny, head_cols
    )
    qkv_shift = lax.dynamic_index_in_dim(qkv_all, gy, 0, keepdims=False)
    mine = lax.dynamic_index_in_dim(lines[:, 3], gx, 1, keepdims=False)
    size = out_bias.shape[0]
    out_cols = mine[:, :size].reshape(part) + mine[:, size : 2 * size].reshape(part)

    full_rows = jnp.stack([g[:sub] for g in gathered]).reshape(rows, width).astype(f32)
    average = jnp.mean(full_rows, axis=-1, keepdims=True)
    centred = full_rows - average
    rate = lax.rsqrt(jnp.mean(centred * centred, axis=-1, keepdims=True) + eps_norm)
    xhat = centred * rate
    normed_attn = (xhat * gain_attn + shift_attn).astype(bf16)
    normed_ffn = (xhat * gain_ffn + shift_ffn).astype(bf16)

    position = (
        block_rows * (jnp.arange(ny, dtype=jnp.int32) ^ gy)[:, None]
        + sub * gx
        + jnp.arange(sub, dtype=jnp.int32)[None]
    ).reshape(rows)
    angles = angle_table(position)
    mixed = jnp.dot(normed_attn, qkv_full, preferred_element_type=f32) + qkv_shift
    mixed = mixed.reshape(rows, 1, 3, HEAD)
    query = (rotate(mixed[:, :, 0], angles).astype(bf16) * jnp.asarray(HEAD ** (-0.5), bf16)).reshape(
        rows, HEAD
    )
    key = rotate(mixed[:, :, 1], angles).astype(bf16).reshape(rows, HEAD)
    value = mixed[:, :, 2].astype(bf16).reshape(rows, HEAD)
    kv = jnp.concatenate([key, value], axis=1)
    kv_parts = gather_gx(kv)
    context, context_low, log_total = attend(where, query, kv_parts)

    hidden_pre = jnp.dot(normed_ffn, up_full, preferred_element_type=f32) + up_shift
    hidden, gelu_back = jax.vjp(exact_gelu, hidden_pre)
    hidden_low = hidden.astype(bf16)
    branch = jnp.dot(hidden_low, down_full, preferred_element_type=f32) + jnp.dot(
        context_low, out_full, preferred_element_type=f32
    )
    mixed_out = scatter_gy(branch.astype(bf16).reshape(ny, sub, width))
    mixed_out = exchange_gx(mixed_out.astype(bf16))
    output = (tokens.astype(f32) + mixed_out.astype(f32) + out_cols).astype(bf16)

    grad_context = contract_last(cot, out_full).astype(bf16)
    grad_hidden = contract_last(cot, down_full)
    grad_pre = gelu_back(grad_hidden)[0].astype(bf16)
    dq, *dkv = attend_back(where, query, grad_context, context, log_total, kv_parts)
    dkv = scatter_gx(dkv)
    spun = [
        unrotate(g.reshape(rows, 1, HEAD), angles).reshape(rows, HEAD) for g in (dq, dkv[:, :HEAD])
    ]
    grad_mixed = jnp.concatenate(spun + [dkv[:, HEAD:]], axis=1).astype(bf16)

    d_up = contract_first(normed_ffn, grad_pre).astype(bf16)
    d_down = contract_first(hidden_low, cot).astype(bf16)
    d_up_b = jnp.sum(grad_pre.astype(f32), axis=0).astype(bf16)
    parts = []
    for m in range(4):
        cols = slice(m * unit, (m + 1) * unit)
        up_piece = d_up[:, cols].reshape(ny, krows, unit)
        down_piece = jnp.transpose(d_down[cols].reshape(unit, ny, krows), (1, 0, 2))
        body = jnp.concatenate([up_piece, down_piece], axis=1).reshape(ny * 2 * krows, unit)
        tail = jnp.pad(d_up_b[cols][None], ((0, 15), (0, 0)))
        parts.append(jnp.concatenate([body, tail]))
    summed = scatter_gx(parts)
    grad_up_b = summed[ny * 2 * krows]
    summed = summed[: ny * 2 * krows].astype(bf16).reshape(ny, 2 * krows, unit)
    summed = lax.all_to_all(summed, "gy", 0, 0, tiled=True)
    grad_up_w = jnp.transpose(summed[:, :krows], (1, 0, 2)).reshape(krows, ny * unit).astype(f32)
    grad_down_w = summed[:, krows:].reshape(ny * unit, krows).astype(f32)

    grad_norm_attn = contract_last(grad_mixed, qkv_full)
    grad_norm_ffn = contract_last(grad_pre, up_full)
    u = (grad_norm_attn * gain_attn + grad_norm_ffn * gain_ffn).astype(bf16)
    sums = jnp.stack(
        [
            jnp.sum(grad_norm_attn * xhat, axis=0),
            jnp.sum(grad_norm_attn, axis=0),
            jnp.sum(grad_norm_ffn * xhat, axis=0),
            jnp.sum(grad_norm_ffn, axis=0),
        ]
    ).reshape(4, ny, krows)
    cot_sum = jnp.sum(cotangent.astype(f32), axis=0).reshape(1, ny, size)
    cot_sum = jnp.pad(cot_sum, ((0, 0), (0, 0), (0, krows - size)))
    rest = jnp.concatenate([sums, cot_sum, jnp.zeros((3, ny, krows), f32)])
    rest = jnp.transpose(rest, (1, 0, 2)).reshape(ny, 1, width).astype(bf16)
    ordered = jnp.concatenate(
        [lax.dynamic_index_in_dim(rest, gy ^ m, 0) for m in range(8)]
    )
    ordered = jnp.pad(ordered, ((0, 0), (0, 15), (0, 0)))
    grouped = jnp.concatenate([u.reshape(ny, sub, width), ordered], axis=1)
    reduced = scatter_gy(grouped)
    u_sum = reduced[:sub]
    flat = reduced[sub].reshape(8, krows)
    grad_bias = flat[4, :size]
    gains = flat[:4].reshape(2, 2 * krows)
    mine_rows = own_rows[:sub].astype(f32)
    centre = mine_rows - jnp.mean(mine_rows, axis=-1, keepdims=True)
    mine_rate = lax.rsqrt(jnp.mean(centre * centre, axis=-1, keepdims=True) + eps_norm)
    mine_xhat = centre * mine_rate
    back = mine_rate * (
        u_sum
        - jnp.mean(u_sum, axis=-1, keepdims=True)
        - mine_xhat * jnp.mean(u_sum * mine_xhat, axis=-1, keepdims=True)
    )
    gain_row = jnp.pad(gains, ((0, 14), (0, 0)))
    blocks = jnp.transpose(back.reshape(sub, nx, part), (1, 0, 2))
    blocks = jnp.concatenate([blocks, jnp.broadcast_to(gain_row[None], (nx, 16, part))], axis=1)
    arrived = lax.all_to_all(blocks.astype(bf16), "gx", 0, 0, tiled=True).astype(f32)
    grad_tokens = cotangent.astype(f32) + arrived[:, :sub].reshape(block_rows, part)
    gain_sum = jnp.sum(arrived[:, sub : sub + 2], axis=0).reshape(4, krows)

    d_qkv = contract_first(normed_attn, grad_mixed).astype(bf16).reshape(ny, krows, head_cols)
    d_out = contract_first(context_low, cot).astype(bf16)
    d_out = jnp.transpose(d_out.reshape(HEAD, ny, krows), (1, 0, 2))
    d_qkv_b = jnp.sum(grad_mixed.astype(f32), axis=0).astype(bf16).reshape(4, bias_size)
    bias_rows = jnp.concatenate([d_qkv_b, d_qkv_b])
    bias_rows = jnp.pad(bias_rows[:, None], ((0, 0), (0, 15), (0, head_cols + krows - bias_size)))
    both = jnp.concatenate([jnp.concatenate([d_qkv, d_out], axis=2), bias_rows], axis=1)
    both = both.reshape((nx, 2) + both.shape[1:])
    reduced_att = scatter_gx(
        [lax.dynamic_index_in_dim(both, gx ^ m, 0, keepdims=False) for m in range(4)]
    ).astype(bf16)
    send = [jnp.where(odd, reduced_att[1 - s], reduced_att[s]) for s in (0, 1)]
    returns = [[(b, a) for a, b in pairs[s]] for s in (0, 1)]
    got = [lax.ppermute(send[s], ("gx", "gy"), returns[s]) for s in (0, 1)]
    by_head = [jnp.where(odd, got[1 - a], got[a]).astype(f32) for a in (0, 1)]
    grad_qkv_w = jnp.concatenate([b[:krows, :head_cols] for b in by_head], axis=1)
    grad_out_w = jnp.concatenate([b[:krows, head_cols:] for b in by_head], axis=0)
    grad_qkv_b = jnp.where(gy < 4, by_head[0][krows, :bias_size], by_head[1][krows, :bias_size])

    return (
        output,
        grad_tokens,
        gain_sum[0],
        gain_sum[1],
        gain_sum[2],
        gain_sum[3],
        grad_qkv_w,
        grad_qkv_b,
        grad_out_w,
        grad_bias,
        grad_up_w,
        grad_up_b,
        grad_down_w,
        grad_bias,
    )


def exchange_gx(rows_block):
    rows, width = rows_block.shape
    count = lax.axis_size("gx")
    pieces = jnp.transpose(rows_block.reshape(rows, count, width // count), (1, 0, 2))
    return lax.all_to_all(pieces, "gx", 0, 0, tiled=True).reshape(count * rows, width // count)


def solution(mesh):
    placed = (
        P("gy", "gx"),
        P("gy"),
        P("gy"),
        P("gy"),
        P("gy"),
        P("gy", "gx"),
        P(("gx", "gy")),
        P("gx", "gy"),
        P(("gx", "gy")),
        P("gy", "gx"),
        P(("gx", "gy")),
        P("gx", "gy"),
        P(("gx", "gy")),
        P("gy", "gx"),
    )
    return jax.shard_map(
        regroup if mesh.shape["gy"] == SPAN and mesh.shape["gx"] == 4 else local,
        mesh=mesh,
        in_specs=placed,
        out_specs=(
            P("gy", "gx"),
            P("gy", "gx"),
            P("gy"),
            P("gy"),
            P("gy"),
            P("gy"),
            P("gy", "gx"),
            P(("gx", "gy")),
            P("gx", "gy"),
            P(("gx", "gy")),
            P("gy", "gx"),
            P(("gx", "gy")),
            P("gx", "gy"),
            P(("gx", "gy")),
        ),
        check_vma=False,
    )
```

```python
import jax
import jax.numpy as jnp
from jax import lax
from jax.experimental import pallas as pl
from jax.experimental.pallas import tpu as pltpu
from jax.sharding import PartitionSpec as P

HEAD = 256
ROT = 64
SPAN = 8


eps_norm = 1e-05


def passed_along(value, axis, steps):
    count = lax.axis_size(axis)
    leading, last = (max(0, -steps), min(count, count - steps))
    return lax.ppermute(value, axis, [(source, source + steps) for source in range(leading, last)])


def norm_rows(values, gain, shift):
    average = jnp.mean(values, axis=-1, keepdims=True)
    centred = values - average
    spread = jnp.mean(centred * centred, axis=-1, keepdims=True)
    return centred * lax.rsqrt(spread + eps_norm) * gain + shift


def exact_gelu(values):
    return jax.nn.gelu(values, approximate=False)


def angle_table(positions):
    half_rot = ROT // 2
    frequency = 10000.0 ** (-(2.0 * jnp.arange(half_rot).astype(jnp.float32)) / ROT)
    return positions.astype(jnp.float32)[:, None] * frequency[None, :]


def rotate(heads, angles):
    half_rot = angles.shape[-1]
    cosine = jnp.cos(angles)[:, None, :]
    sine = jnp.sin(angles)[:, None, :]
    first = heads[..., :half_rot]
    second = heads[..., half_rot : 2 * half_rot]
    return jnp.concatenate(
        [
            first * cosine - second * sine,
            second * cosine + first * sine,
            heads[..., 2 * half_rot :],
        ],
        axis=-1,
    )


def unrotate(heads, angles):
    half_rot = angles.shape[-1]
    cosine = jnp.cos(angles)[:, None, :]
    sine = jnp.sin(angles)[:, None, :]
    first = heads[..., :half_rot]
    second = heads[..., half_rot : 2 * half_rot]
    return jnp.concatenate(
        [
            first * cosine + second * sine,
            second * cosine - first * sine,
            heads[..., 2 * half_rot :],
        ],
        axis=-1,
    )


def contract_last(left, right):
    return lax.dot_general(
        left, right, (((1,), (1,)), ((), ())), preferred_element_type=jnp.float32
    )


def contract_first(left, right):
    return lax.dot_general(
        left, right, (((0,), (0,)), ((), ())), preferred_element_type=jnp.float32
    )


def visible_mask(query_pos, key_pos, seq_len):
    return (
        (key_pos[None, :] <= query_pos[:, None])
        & (key_pos >= 0)[None, :]
        & (query_pos < seq_len)[:, None]
    )


def pair_grads(
    query_set, grad_set, log_total, delta, query_pos, key_set, value_set, key_pos, seq_len
):
    factor = HEAD ** (-0.5)
    scores = (
        jnp.einsum("qhd,khd->hqk", query_set, key_set, preferred_element_type=jnp.float32) * factor
    )
    visible = visible_mask(query_pos, key_pos, seq_len)
    probs = jnp.where(
        visible[None], jnp.exp(jnp.where(visible[None], scores - log_total[:, :, None], 0.0)), 0.0
    )
    grad_probs = jnp.einsum("qhd,khd->hqk", grad_set, value_set, preferred_element_type=jnp.float32)
    grad_scores = (probs * (grad_probs - delta[:, :, None])).astype(jnp.bfloat16)
    grad_q = (
        jnp.einsum("hqk,khd->qhd", grad_scores, key_set, preferred_element_type=jnp.float32)
        * factor
    )
    grad_k = (
        jnp.einsum("hqk,qhd->khd", grad_scores, query_set, preferred_element_type=jnp.float32)
        * factor
    )
    grad_v = jnp.einsum(
        "hqk,qhd->khd", probs.astype(jnp.bfloat16), grad_set, preferred_element_type=jnp.float32
    )
    return (grad_q, grad_k, grad_v)


def local(
    tokens,
    attn_gain,
    attn_shift,
    ffn_gain,
    ffn_shift,
    qkv_weight,
    qkv_bias,
    out_weight,
    out_bias,
    up_weight,
    up_bias,
    down_weight,
    down_bias,
    cotangent,
):
    tok_rows = tokens.shape[0]
    width_part = tokens.shape[1]
    local_heads = qkv_weight.shape[1] // (3 * HEAD)
    factor = HEAD ** (-0.5)
    seq_len = tok_rows * SPAN
    local_start = lax.axis_index("gy") % SPAN * tok_rows
    positions = local_start + jnp.arange(tok_rows, dtype=jnp.int32)
    angles = angle_table(positions)
    full_rows = lax.all_gather(tokens, "gx", axis=1, tiled=True).astype(jnp.float32)
    qkv_full, up_full, qkv_shift, up_shift, gain_attn, shift_attn, gain_ffn, shift_ffn = (
        lax.all_gather(qkv_weight, "gy", axis=0, tiled=True),
        lax.all_gather(up_weight, "gy", axis=0, tiled=True),
        lax.all_gather(qkv_bias, "gy", axis=0, tiled=True),
        lax.all_gather(up_bias, "gy", axis=0, tiled=True),
        lax.all_gather(attn_gain, "gy", axis=0, tiled=True),
        lax.all_gather(attn_shift, "gy", axis=0, tiled=True),
        lax.all_gather(ffn_gain, "gy", axis=0, tiled=True),
        lax.all_gather(ffn_shift, "gy", axis=0, tiled=True),
    )
    normed_attn, back_attn = jax.vjp(
        norm_rows, full_rows, gain_attn.astype(jnp.float32), shift_attn.astype(jnp.float32)
    )
    normed_ffn, back_ffn = jax.vjp(
        norm_rows, full_rows, gain_ffn.astype(jnp.float32), shift_ffn.astype(jnp.float32)
    )
    normed_attn = normed_attn.astype(jnp.bfloat16)
    normed_ffn = normed_ffn.astype(jnp.bfloat16)
    mixed = jnp.dot(normed_attn, qkv_full, preferred_element_type=jnp.float32) + qkv_shift.astype(
        jnp.float32
    )
    mixed = mixed.reshape(tok_rows, local_heads, 3, HEAD)
    queries = rotate(mixed[:, :, 0], angles).astype(jnp.bfloat16)
    keys = rotate(mixed[:, :, 1], angles).astype(jnp.bfloat16)
    values = mixed[:, :, 2].astype(jnp.bfloat16)
    head_cols = local_heads * HEAD

    def attend_piece(carried, piece_keys, piece_values, offset):
        row_max, row_total, summed = carried
        length = piece_keys.shape[0]
        scores = (
            jnp.einsum("qhd,khd->hqk", queries, piece_keys, preferred_element_type=jnp.float32)
            * factor
        )
        visible = visible_mask(positions, offset + jnp.arange(length, dtype=jnp.int32), seq_len)
        scores = jnp.where(visible[None], scores, -1e30)
        new_max = jnp.maximum(row_max, jnp.max(scores, axis=-1))
        weights = jnp.where(visible[None], jnp.exp(scores - new_max[:, :, None]), 0.0)
        shrink = jnp.exp(row_max - new_max)
        row_total = row_total * shrink + jnp.sum(weights, axis=-1)
        summed = summed * jnp.transpose(shrink)[:, :, None] + jnp.einsum(
            "hqk,khd->qhd",
            weights.astype(jnp.bfloat16),
            piece_values,
            preferred_element_type=jnp.float32,
        )
        return (new_max, row_total, summed)

    start_state = (
        jnp.full((local_heads, tok_rows), -1e30, jnp.float32),
        jnp.zeros((local_heads, tok_rows), jnp.float32),
        jnp.zeros((tok_rows, local_heads, HEAD), jnp.float32),
    )
    state = attend_piece(start_state, keys, values, local_start)
    kv_stack = jnp.stack(
        [keys.reshape(tok_rows, head_cols), values.reshape(tok_rows, head_cols)], axis=0
    )
    for step in range(1, SPAN):
        arrived = passed_along(kv_stack, "gy", step)
        state = attend_piece(
            state,
            arrived[0].reshape(tok_rows, local_heads, HEAD),
            arrived[1].reshape(tok_rows, local_heads, HEAD),
            local_start - step * tok_rows,
        )
    row_max, row_total, summed = state
    log_total = row_max + jnp.log(row_total)
    context_sum = summed / jnp.transpose(row_total)[:, :, None]
    context_low = context_sum.reshape(tok_rows, head_cols).astype(jnp.bfloat16)
    out_full, down_full, out_cols, down_cols = (
        lax.all_gather(out_weight, "gy", axis=1, tiled=True),
        lax.all_gather(down_weight, "gy", axis=1, tiled=True),
        lax.all_gather(out_bias, "gy", axis=0, tiled=True),
        lax.all_gather(down_bias, "gy", axis=0, tiled=True),
    )
    hidden_pre = jnp.dot(normed_ffn, up_full, preferred_element_type=jnp.float32) + up_shift.astype(
        jnp.float32
    )
    hidden, gelu_back = jax.vjp(exact_gelu, hidden_pre)
    hidden_low = hidden.astype(jnp.bfloat16)
    branch_sum = jnp.dot(context_low, out_full, preferred_element_type=jnp.float32) + jnp.dot(
        hidden_low, down_full, preferred_element_type=jnp.float32
    )
    mixed_out = lax.psum_scatter(
        branch_sum.astype(jnp.bfloat16), "gx", scatter_dimension=1, tiled=True
    ).astype(jnp.float32)
    output = (
        tokens.astype(jnp.float32)
        + mixed_out
        + out_cols.astype(jnp.float32)
        + down_cols.astype(jnp.float32)
    ).astype(jnp.bfloat16)
    grad_rows = lax.all_gather(cotangent, "gx", axis=1, tiled=True)
    grad_context = contract_last(grad_rows, out_full).astype(jnp.bfloat16)
    grad_hidden = contract_last(grad_rows, down_full)
    grad_pre = gelu_back(grad_hidden)[0].astype(jnp.bfloat16)
    grad_out_local = contract_first(context_low, grad_rows)
    grad_down_local = contract_first(hidden_low, grad_rows)
    grad_bias_cols = jnp.sum(cotangent.astype(jnp.float32), axis=0)
    grad_out_w, grad_down_w, grad_bias = (
        lax.psum_scatter(
            grad_out_local.astype(jnp.bfloat16), "gy", scatter_dimension=1, tiled=True
        ).astype(jnp.float32),
        lax.psum_scatter(
            grad_down_local.astype(jnp.bfloat16), "gy", scatter_dimension=1, tiled=True
        ).astype(jnp.float32),
        lax.psum_scatter(
            grad_bias_cols.astype(jnp.bfloat16), "gy", scatter_dimension=0, tiled=True
        ).astype(jnp.float32),
    )
    grad_heads = grad_context.reshape(tok_rows, local_heads, HEAD)
    delta = jnp.einsum("qhd,qhd->hq", grad_heads.astype(jnp.float32), context_sum)
    grad_q, grad_k, grad_v = pair_grads(
        queries, grad_heads, log_total, delta, positions, keys, values, positions, seq_len
    )
    row_stack = jnp.stack(
        [
            queries.reshape(tok_rows, head_cols),
            grad_context,
            keys.reshape(tok_rows, head_cols),
            values.reshape(tok_rows, head_cols),
        ],
        axis=0,
    )
    stat_stack = jnp.stack([log_total, delta], axis=0)
    for step in [item for item in range(1 - SPAN, SPAN) if item != 0]:
        arrived = passed_along(row_stack, "gy", step)
        stats = passed_along(stat_stack, "gy", step)
        piece_pos = local_start - step * tok_rows + jnp.arange(tok_rows, dtype=jnp.int32)
        other_q = arrived[0].reshape(tok_rows, local_heads, HEAD)
        other_g = arrived[1].reshape(tok_rows, local_heads, HEAD)
        other_k = arrived[2].reshape(tok_rows, local_heads, HEAD)
        other_v = arrived[3].reshape(tok_rows, local_heads, HEAD)
        if step > 0:
            part_q, unused_k, unused_v = pair_grads(
                queries,
                grad_heads,
                log_total,
                delta,
                positions,
                other_k,
                other_v,
                piece_pos,
                seq_len,
            )
            grad_q = grad_q + part_q
        else:
            unused_q, part_k, part_v = pair_grads(
                other_q, other_g, stats[0], stats[1], piece_pos, keys, values, positions, seq_len
            )
            grad_k = grad_k + part_k
            grad_v = grad_v + part_v
    grad_mixed = jnp.stack([unrotate(grad_q, angles), unrotate(grad_k, angles), grad_v], axis=2)
    grad_mixed = grad_mixed.reshape(tok_rows, 3 * head_cols).astype(jnp.bfloat16)
    grad_norm_attn = contract_last(grad_mixed, qkv_full)
    grad_norm_ffn = contract_last(grad_pre, up_full)
    sum_attn, sum_ffn = (
        lax.psum(grad_norm_attn.astype(jnp.bfloat16), "gx").astype(jnp.float32),
        lax.psum(grad_norm_ffn.astype(jnp.bfloat16), "gx").astype(jnp.float32),
    )
    input_attn, gain_grad_attn, shift_grad_attn = back_attn(sum_attn)
    input_ffn, gain_grad_ffn, shift_grad_ffn = back_ffn(sum_ffn)
    own_cols = lax.dynamic_slice_in_dim(
        input_attn + input_ffn, lax.axis_index("gx") * width_part, width_part, 1
    )
    grad_tokens = cotangent.astype(jnp.float32) + own_cols
    grad_qkv_local = contract_first(normed_attn, grad_mixed)
    grad_up_local = contract_first(normed_ffn, grad_pre)
    grad_qkv_cols = jnp.sum(grad_mixed.astype(jnp.float32), axis=0)
    grad_up_cols = jnp.sum(grad_pre.astype(jnp.float32), axis=0)
    (
        grad_qkv_w,
        grad_up_w,
        grad_qkv_b,
        grad_up_b,
        grad_gain_attn,
        grad_shift_attn,
        grad_gain_ffn,
        grad_shift_ffn,
    ) = (
        lax.psum_scatter(
            grad_qkv_local.astype(jnp.bfloat16), "gy", scatter_dimension=0, tiled=True
        ).astype(jnp.float32),
        lax.psum_scatter(
            grad_up_local.astype(jnp.bfloat16), "gy", scatter_dimension=0, tiled=True
        ).astype(jnp.float32),
        lax.psum_scatter(
            grad_qkv_cols.astype(jnp.bfloat16), "gy", scatter_dimension=0, tiled=True
        ).astype(jnp.float32),
        lax.psum_scatter(
            grad_up_cols.astype(jnp.bfloat16), "gy", scatter_dimension=0, tiled=True
        ).astype(jnp.float32),
        lax.psum_scatter(
            gain_grad_attn.astype(jnp.bfloat16), "gy", scatter_dimension=0, tiled=True
        ).astype(jnp.float32),
        lax.psum_scatter(
            shift_grad_attn.astype(jnp.bfloat16), "gy", scatter_dimension=0, tiled=True
        ).astype(jnp.float32),
        lax.psum_scatter(
            gain_grad_ffn.astype(jnp.bfloat16), "gy", scatter_dimension=0, tiled=True
        ).astype(jnp.float32),
        lax.psum_scatter(
            shift_grad_ffn.astype(jnp.bfloat16), "gy", scatter_dimension=0, tiled=True
        ).astype(jnp.float32),
    )
    return (
        output,
        grad_tokens,
        grad_gain_attn,
        grad_shift_attn,
        grad_gain_ffn,
        grad_shift_ffn,
        grad_qkv_w,
        grad_qkv_b,
        grad_out_w,
        grad_bias,
        grad_up_w,
        grad_up_b,
        grad_down_w,
        grad_bias,
    )


MESH = pl.DeviceIdType.MESH
NX = 4
NY = 8


class Place:
    def __init__(self):
        self.gx, self.gy = lax.axis_index("gx"), lax.axis_index("gy")
        self.z, self.y = self.gy // 2, self.gy % 2
        self.near = self.gx + 1 - 2 * (self.gx % 2)
        self.far = (self.gx + 2) % NX
        self.over = (self.near + 2) % NX
        self.side = self.gy + 1 - 2 * self.y

    def up(self, step):
        return ((self.z + step) % 4) * 2 + self.y


class Post:
    def __init__(self, send, recv):
        self.send, self.recv, self.used = send, recv, 0
        self.open = []

    def take(self, count=1):
        first = self.used
        self.used += count
        return first

    def copy(self, slot, src, dst, gx, gy, offset=None):
        index = slot if offset is None else slot + offset
        return pltpu.make_async_remote_copy(
            src_ref=src,
            dst_ref=dst,
            send_sem=self.send.at[slot],
            recv_sem=self.recv.at[index],
            device_id=(gx, gy),
            device_id_type=MESH,
        )

    def go(self, *args, **kw):
        made = self.copy(*args, **kw)
        made.start()
        self.open.append(made)
        return made

    def arrived(self, slot, dst, gx, gy):
        self.copy(slot, dst, dst, gx, gy).wait_recv()

    def close(self):
        for made in self.open:
            made.wait_send()
        self.open = []


def greet(peers):
    barrier = pltpu.get_barrier_semaphore()
    for gx, gy in peers:
        pl.semaphore_signal(barrier, inc=1, device_id=(gx, gy), device_id_type=MESH)
    pl.semaphore_wait(barrier, len(peers))


def greet_all(here):
    barrier = pltpu.get_barrier_semaphore()
    gx, gy = here.gx, here.gy
    peers = [((gx + s) % NX, gy) for s in range(1, NX)]
    peers += [(gx, (gy + s) % NY) for s in range(1, NY)]
    for px, py in peers:
        pl.semaphore_signal(barrier, inc=1, device_id=(px, py), device_id_type=MESH)
    peers = [(here.z, 2 * gx), (here.z, 2 * gx + 1)]
    for px, py in peers:
        pl.semaphore_signal(barrier, inc=1, device_id=(px, py), device_id_type=MESH)
    pl.semaphore_wait(barrier, NX + NY)
    return here.z == gx


def row_spread(post, here, src, dst, local_sem):
    sub, part = dst.shape[0], src.shape[1]
    slot = post.take(NX)
    own = pltpu.make_async_copy(
        src.at[pl.ds(pl.multiple_of(here.gx * sub, sub), sub)],
        dst.at[:, pl.ds(pl.multiple_of(here.gx * part, part), part)],
        local_sem,
    )
    own.start()
    for step in range(1, NX):
        to = (here.gx + step) % NX
        post.go(
            slot + step,
            src.at[pl.ds(pl.multiple_of(to * sub, sub), sub)],
            dst.at[:, pl.ds(pl.multiple_of(here.gx * part, part), part)],
            to,
            here.gy,
        )

    def wait():
        own.wait()
        for step in range(1, NX):
            came = (here.gx + NX - step) % NX
            post.arrived(
                slot + step, dst.at[:, pl.ds(pl.multiple_of(came * part, part), part)], came, here.gy
            )

    return wait


def small_spread(post, here, src, dst, local_sem):
    part = src.shape[1]
    slot = post.take(NX)
    mine = dst.at[:, pl.ds(pl.multiple_of(here.gx * part, part), part)]
    own = pltpu.make_async_copy(src, mine, local_sem)
    own.start()
    for step in range(1, NX):
        post.go(slot + step, src, mine, (here.gx + step) % NX, here.gy)

    def wait():
        own.wait()
        for step in range(1, NX):
            came = (here.gx + NX - step) % NX
            post.arrived(
                slot + step, dst.at[:, pl.ds(pl.multiple_of(came * part, part), part)], came, here.gy
            )

    return wait


def line_gather(post, here, blocks):
    ups, downs, ys = post.take(3), post.take(3), post.take(7)
    z, y, gx = here.z, here.y, here.gx

    def at(line):
        return blocks.at[line * 2 + y]

    def send(step, way, wait):
        line = z - way * step
        first = ups if way > 0 else downs
        made = post.copy(first + step, at(line), at(line), gx, (z + way) * 2 + y)
        ok = jnp.logical_and(
            jnp.logical_and(line >= 0, line <= 3), (z < 3) if way > 0 else (z > 0)
        )

        @pl.when(ok)
        def _():
            made.wait_send() if wait else made.start()

    def come(step, way):
        line = z - way * step
        first = ups if way > 0 else downs
        made = post.copy(first + step - 1, at(line), at(line), gx, here.side)
        on = post.copy(ys + 2 * step - (way > 0), at(line), at(line), gx, here.side)
        ok = (line >= 0) if way > 0 else (line <= 3)

        @pl.when(ok)
        def _():
            made.wait_recv()
            on.start()

    own = post.copy(ys, at(z), at(z), gx, here.side)
    send(0, 1, False)
    send(0, -1, False)
    own.start()

    def relay(step):
        come(step, 1)
        come(step, -1)
        if step < 3:
            send(step, 1, False)
            send(step, -1, False)

    def wait():
        own.wait_send()
        post.copy(ys, at(z), blocks.at[here.side], gx, here.side).wait_recv()
        for step in (0, 1, 2):
            send(step, 1, True)
            send(step, -1, True)
        for step in (1, 2, 3):
            for way in (1, -1):
                line = z - way * step
                ok = (line >= 0) if way > 0 else (line <= 3)
                slot = ys + 2 * step - (way > 0)

                @pl.when(ok)
                def _():
                    post.copy(slot, at(line), at(line), gx, here.side).wait_send()
                    post.copy(
                        slot, at(line), blocks.at[line * 2 + 1 - y], gx, here.side
                    ).wait_recv()

    return relay, wait


def gather_kernel(tok, small, cot, qkv, outw, up, down, xb, cb, wq, wo, uu, dd, send, recv, fsend, frecv, loc):
    here = Place()
    post = Post(send, recv)
    gx, gy = here.gx, here.gy
    width3 = wq.shape[2]
    head = wo.shape[1]
    unit = uu.shape[2]
    selfish = greet_all(here)
    sub = cb.shape[1]
    tok_wait = row_spread(post, here, tok, xb.at[gy, 0:sub], loc.at[0])
    small_wait = small_spread(post, here, small, xb.at[gy, sub : sub + 16], loc.at[1])
    att = post.take(4)
    for t in (0, 1):
        alone = jnp.logical_and(selfish, here.y == t)
        for k, (src, dst) in enumerate(
            (
                (qkv.at[:, t * width3 : (t + 1) * width3], wq.at[gy]),
                (outw.at[t * head : (t + 1) * head, :], wo.at[gy]),
            )
        ):
            @pl.when(alone)
            def _():
                pltpu.make_async_copy(src, dst, loc.at[2 + k]).start()

            @pl.when(jnp.logical_not(alone))
            def _():
                pltpu.make_async_remote_copy(
                    src_ref=src,
                    dst_ref=dst,
                    send_sem=send.at[att + 2 * t + k],
                    recv_sem=recv.at[att + 2 * here.y + k],
                    device_id=(here.z, 2 * gx + t),
                    device_id_type=MESH,
                ).start()
    cot_wait = row_spread(post, here, cot, cb.at[gy], loc.at[4])
    tok_wait()
    small_wait()
    tok_relay, tok_done = line_gather(post, here, xb)
    for t in (0, 1):
        alone = jnp.logical_and(selfish, here.y == t)
        for k, (src, dst) in enumerate(
            (
                (qkv.at[:, t * width3 : (t + 1) * width3], wq),
                (outw.at[t * head : (t + 1) * head, :], wo),
            )
        ):
            @pl.when(alone)
            def _():
                pltpu.make_async_copy(src, dst.at[gy], loc.at[2 + k]).wait()

            @pl.when(jnp.logical_not(alone))
            def _():
                slot = dst.at[2 * gx + t]
                made = pltpu.make_async_remote_copy(
                    src_ref=src,
                    dst_ref=slot,
                    send_sem=send.at[att + 2 * t + k],
                    recv_sem=recv.at[att + 2 * t + k],
                    device_id=(here.z, 2 * gx + t),
                    device_id_type=MESH,
                )
                made.wait_send()
                made.wait_recv()
    att_far, att_near, att_over = post.take(2), post.take(2), post.take(2)
    for k, w in enumerate((wq, wo)):
        pair = w.at[pl.ds(2 * gx, 2)]
        post.go(att_far + k, pair, pair, here.far, gy)
        post.go(att_near + k, pair, pair, here.near, gy)
    for hop in (1, 2, 3):
        tok_relay(hop)
    mine_u = uu.at[gx]
    mine_d = dd.at[gx]
    own_u = pltpu.make_async_copy(
        up.at[:, pl.ds(pl.multiple_of(gy * unit, unit), unit)],
        mine_u.at[pl.ds(pl.multiple_of(gy * unit, unit), unit)],
        loc.at[5],
    )
    own_d = pltpu.make_async_copy(
        down.at[pl.ds(pl.multiple_of(gy * unit, unit), unit), :],
        mine_d.at[:, pl.ds(pl.multiple_of(gy * unit, unit), unit)],
        loc.at[6],
    )
    own_u.start()
    own_d.start()

    def ffn(k, step, to):
        place = pl.ds(pl.multiple_of(gy * unit, unit), unit)
        theirs = pl.ds(pl.multiple_of(to * unit, unit), unit)
        src = up.at[:, theirs] if k == 0 else down.at[theirs, :]
        dst = mine_u.at[place] if k == 0 else mine_d.at[:, place]
        return pltpu.make_async_remote_copy(
            src_ref=src, dst_ref=dst, send_sem=fsend.at[k, step], recv_sem=frecv.at[k, gy],
            device_id=(gx, to), device_id_type=MESH,
        )

    for step in range(1, NY):
        for k in (0, 1):
            ffn(k, step, (gy + step) % NY).start()
    cot_wait()
    cot_relay, cot_done = line_gather(post, here, cb)
    for k, w in enumerate((wq, wo)):
        pair = w.at[pl.ds(2 * here.far, 2)]
        post.arrived(att_far + k, pair, here.far, gy)
        post.go(att_over + k, pair, pair, here.near, gy)

    def piece(k, part, q):
        place = pl.ds(pl.multiple_of(q * unit, unit), unit)
        return uu.at[part, place] if k == 0 else dd.at[part, :, place]

    def pass_on(k, row, part, q, to):
        ref = piece(k, part, q)
        return pltpu.make_async_remote_copy(
            src_ref=ref, dst_ref=ref, send_sem=fsend.at[row, q], recv_sem=frecv.at[row, q],
            device_id=(to, gy), device_id_type=MESH,
        )

    own_u.wait()
    own_d.wait()

    def first(q, carried):
        for k in (0, 1):
            @pl.when(q != gy)
            def _():
                ref = piece(k, gx, q)
                pltpu.make_async_remote_copy(
                    src_ref=ref, dst_ref=ref, send_sem=fsend.at[k, 0], recv_sem=frecv.at[k, q],
                    device_id=(gx, q), device_id_type=MESH,
                ).wait_recv()
            pass_on(k, 2 + k, gx, q, here.far).start()
            pass_on(k, 4 + k, gx, q, here.near).start()
        return carried

    lax.fori_loop(0, NY, first, 0)
    cot_relay(1)
    cot_relay(2)

    def second(q, carried):
        for k in (0, 1):
            pass_on(k, 2 + k, here.far, q, here.far).wait_recv()
            pass_on(k, 6 + k, here.far, q, here.near).start()
        return carried

    cot_relay(3)
    lax.fori_loop(0, NY, second, 0)
    tok_done()
    cot_done()
    for k, w in enumerate((wq, wo)):
        post.arrived(att_near + k, w.at[pl.ds(2 * here.near, 2)], here.near, gy)
        post.arrived(att_over + k, w.at[pl.ds(2 * here.over, 2)], here.near, gy)

    def third(q, carried):
        for k in (0, 1):
            pass_on(k, 4 + k, here.near, q, here.near).wait_recv()
            pass_on(k, 6 + k, here.over, q, here.near).wait_recv()
            pass_on(k, 2 + k, gx, q, here.far).wait_send()
            pass_on(k, 4 + k, gx, q, here.near).wait_send()
            pass_on(k, 6 + k, here.far, q, here.near).wait_send()
        return carried

    lax.fori_loop(0, NY, third, 0)
    for step in range(1, NY):
        for k in (0, 1):
            ffn(k, step, (gy + step) % NY).wait_send()
    post.close()


def gather_all(tokens, small, cotangent, qkv_weight, out_weight, up_weight, down_weight):
    block_rows, part = tokens.shape
    sub = block_rows // NX
    width = part * NX
    krows = qkv_weight.shape[0]
    bf16 = jnp.bfloat16
    unit = up_weight.shape[1] // NY
    vm = pl.BlockSpec(memory_space=pltpu.VMEM)
    hb = pl.BlockSpec(memory_space=pl.ANY)
    return pl.pallas_call(
        gather_kernel,
        out_shape=[
            jax.ShapeDtypeStruct((NY, sub + 16, width), bf16),
            jax.ShapeDtypeStruct((NY, sub, width), bf16),
            jax.ShapeDtypeStruct((NY, krows, qkv_weight.shape[1] // 2), bf16),
            jax.ShapeDtypeStruct((NY, out_weight.shape[0] // 2, out_weight.shape[1]), bf16),
            jax.ShapeDtypeStruct((NX, width, unit), bf16),
            jax.ShapeDtypeStruct((NX, unit, width), bf16),
        ],
        in_specs=[hb] * 7,
        out_specs=[vm] * 6,
        scratch_shapes=[
            pltpu.SemaphoreType.DMA((48,)),
            pltpu.SemaphoreType.DMA((48,)),
            pltpu.SemaphoreType.DMA((8, 8)),
            pltpu.SemaphoreType.DMA((8, 8)),
            pltpu.SemaphoreType.DMA((8,)),
        ],
        compiler_params=pltpu.CompilerParams(
            collective_id=0, has_side_effects=True, vmem_limit_bytes=50 * 2**20
        ),
        name="gather_all",
    )(tokens, small, cotangent, qkv_weight, out_weight, up_weight, down_weight)


def over_rows(count, width, fn):
    chunk = 16
    while 2 * chunk * width <= 65536 and count % (2 * chunk) == 0:
        chunk *= 2

    def body(index, carried):
        fn(pl.ds(pl.multiple_of(index * chunk, chunk), chunk))
        return carried

    lax.fori_loop(0, count // chunk, body, 0)


def shifted(rows, offset):
    return pl.ds(pl.multiple_of(rows.start + offset, 16), rows.size)


class Reduce:
    def __init__(self, post, here, load, full, near, mine, sent, came):
        self.post, self.here = post, here
        self.near, self.mine, self.sent, self.came = near, mine, sent, came
        self.rows, self.width = sent.shape
        self.slot = post.take(2)
        self.far = post.take(1)
        rows = self.rows
        group = lambda p: full.at[pl.ds(pl.multiple_of(p * rows, rows), rows)]
        for k, p in enumerate((here.near, here.over)):
            post.go(self.slot + k, group(p), near.at[k * rows : (k + 1) * rows], here.near, here.gy)
        self.loads = [
            load(group(p), mine.at[k * rows : (k + 1) * rows])
            for k, p in enumerate((here.gx, here.far))
        ]

    def cross(self):
        rows = self.rows
        self.loads[1].wait()
        self.post.arrived(
            self.slot + 1, self.near.at[rows : 2 * rows], self.here.near, self.here.gy
        )

        def add(r):
            low = shifted(r, rows)
            self.sent[r] = (
                self.mine[low].astype(jnp.float32) + self.near[low].astype(jnp.float32)
            ).astype(jnp.bfloat16)

        over_rows(rows, self.width, add)
        self.post.go(self.far, self.sent, self.came, self.here.far, self.here.gy)

    def total(self, put):
        rows = self.rows
        self.loads[0].wait()
        self.post.arrived(self.slot, self.near.at[0:rows], self.here.near, self.here.gy)
        self.post.arrived(self.far, self.came, self.here.far, self.here.gy)

        def add(r):
            put(
                r,
                self.mine[r].astype(jnp.float32)
                + self.near[r].astype(jnp.float32)
                + self.came[r].astype(jnp.float32),
            )

        over_rows(rows, self.width, add)


def scatter_kernel(
    bo, ug, dq, do, qb, du, dd, ub, own, tok, cot, cols,
    output, grad_tokens, gains, smalls, gup, gdown, gqkv, gout, gqb, gub,
    half, come, stage, uhalf, ucome, ustage,
    nq, no, nqb, nu, nd, nub, kq, ko, kqb, ku, kd, kub, fq, fo, fqb, fu, fd, fub,
    rq, ro, rqb, ru, rd, rub, au, ad, aq, ao, ab, mixed, mixed_land, back, back_land,
    send, recv, fsend, frecv, loc,
):
    here = Place()
    gx, gy, z, y = here.gx, here.gy, here.z, here.y
    post = Post(send, recv)
    f32, bf16 = jnp.float32, jnp.bfloat16
    selfish = greet_all(here)
    locs = [0]

    def load(src, dst):
        made = pltpu.make_async_copy(src, dst, loc.at[locs[0]])
        locs[0] += 1
        made.start()
        return made

    def reduce(*refs):
        return Reduce(post, here, load, *refs)

    red_q = reduce(dq, nq, kq, fq, rq)
    red_o = reduce(do, no, ko, fo, ro)
    red_b = reduce(qb, nqb, kqb, fqb, rqb)
    red_u = reduce(du, nu, ku, fu, ru)
    red_d = reduce(dd, nd, kd, fd, rd)
    red_c = reduce(ub, nub, kub, fub, rub)
    ys = []
    for src, mine, land in ((bo, half, come), (ug, uhalf, ucome)):
        slot = post.take(4)
        for k in range(4):
            post.go(slot + k, src.at[2 * k + 1 - y], land.at[k], gx, here.side)
        ys.append((slot, [load(src.at[2 * k + y], mine.at[k]) for k in range(4)]))
    for red in (red_q, red_o, red_b, red_u, red_d, red_c):
        red.cross()

    zs = []
    for (slot, made), mine, land, arrive in (
        (ys[0], half, come, stage),
        (ys[1], uhalf, ucome, ustage),
    ):
        for k in range(4):
            made[k].wait()
            post.arrived(slot + k, land.at[k], gx, here.side)
        first = post.take(4)
        zs.append(first)
        rows, width = mine.shape[1:]
        for step in (1, 2, 3):
            to = (z + step) % 4

            def add(r):
                mine[to, r] = (mine[to, r].astype(f32) + land[to, r].astype(f32)).astype(bf16)

            over_rows(rows, width, add)
            post.go(first + step, mine.at[to], arrive.at[step - 1], gx, to * 2 + y)

    for red, keep in ((red_q, kq), (red_o, ko), (red_b, kqb)):

        def put(r, value):
            keep[r] = value.astype(bf16)

        red.total(put)
    att = post.take(6)
    trio = ((kq, aq), (ko, ao), (kqb, ab))

    def row_pair(ref, t, out):
        rows = out.shape[1]
        return ref.at[t * rows : (t + 1) * rows]

    for t in (0, 1):
        alone = jnp.logical_and(selfish, y == t)
        for k, (mine, out) in enumerate(trio):

            @pl.when(alone)
            def _():
                made = pltpu.make_async_copy(row_pair(mine, t, out), out.at[t], loc.at[40 + k])
                made.start()
                made.wait()

            @pl.when(jnp.logical_not(alone))
            def _():
                pltpu.make_async_remote_copy(
                    src_ref=row_pair(mine, t, out), dst_ref=out.at[y],
                    send_sem=send.at[att + 3 * t + k], recv_sem=recv.at[att + 3 * y + k],
                    device_id=(z, 2 * gx + t), device_id_type=MESH,
                ).start()

    unit = au.shape[0]
    place = pl.ds(pl.multiple_of(gy * unit, unit), unit)
    for k, (red, mine) in enumerate(((red_u, ku), (red_d, kd))):

        def put(r, value):
            mine[r] = value.astype(bf16)

        red.total(put)
        for step in range(1, NY):
            to = (gy + step) % NY
            theirs = pl.ds(pl.multiple_of(to * unit, unit), unit)
            pltpu.make_async_remote_copy(
                src_ref=mine.at[theirs] if k == 0 else mine.at[0:unit, theirs],
                dst_ref=au.at[:, place] if k == 0 else ad.at[place],
                send_sem=fsend.at[k, step], recv_sem=frecv.at[k, step],
                device_id=(gx, to), device_id_type=MESH,
            ).start()
        if k == 0:
            gup[:, place] = mine[place].astype(f32)
        else:
            gdown[place] = mine[0:unit, place].astype(f32)

    def put_b(r, value):
        gub[r] = value

    red_c.total(put_b)

    sub, width = own.shape
    part = width // NX

    def summed(n, mine, land, arrive, r):
        total = mine[z, r].astype(f32) + land[z, r].astype(f32)
        for step in (1, 2, 3):
            total = total + arrive[step - 1, r].astype(f32)
        return total

    def await_z(n, arrive):
        for step in (1, 2, 3):
            post.arrived(zs[n] + step, arrive.at[step - 1], gx, ((z + 4 - step) % 4) * 2 + y)

    await_z(0, stage)

    def put_mixed(r):
        total = summed(0, half, come, stage, r).astype(bf16)
        for p in range(NX):
            mixed[p, r] = total[:, p * part : (p + 1) * part]

    over_rows(sub, 4 * width, put_mixed)
    xs = post.take(4)
    for step in range(1, NX):
        to = (gx + step) % NX
        post.go(xs + step, mixed.at[to], mixed_land.at[step - 1], to, gy)
    await_z(1, ustage)

    def put_back(r):
        rows = summed(1, uhalf, ucome, ustage, r)
        tokens = own[r].astype(f32)
        centred = tokens - jnp.mean(tokens, axis=-1, keepdims=True)
        rate = lax.rsqrt(jnp.mean(centred * centred, axis=-1, keepdims=True) + eps_norm)
        xhat = centred * rate
        grads = rate * (
            rows
            - jnp.mean(rows, axis=-1, keepdims=True)
            - xhat * jnp.mean(rows * xhat, axis=-1, keepdims=True)
        )
        grads = grads.astype(bf16)
        for p in range(NX):
            back[p, r] = grads[:, p * part : (p + 1) * part]

    over_rows(sub, 4 * width, put_back)
    rest = summed(1, uhalf, ucome, ustage, pl.ds(sub, 16))
    smalls[...] = rest
    low = rest.astype(bf16)
    for p in range(NX):
        for q in (0, 1):
            back[p, sub + 16 * q : sub + 16 * (q + 1)] = low[:, q * part : (q + 1) * part]
    us = post.take(4)
    for step in range(1, NX):
        to = (gx + step) % NX
        post.go(us + step, back.at[to], back_land.at[step - 1], to, gy)

    def rows_of(p):
        return pl.multiple_of(p * sub, sub)

    def put_output(p, block):
        def put(r):
            there = shifted(r, rows_of(p))
            output[there] = (tok[there].astype(f32) + block[r].astype(f32) + cols[...]).astype(bf16)

        over_rows(sub, 2 * part, put)

    put_output(gx, mixed.at[gx])
    for step in range(1, NX):
        came = (gx + NX - step) % NX
        post.arrived(xs + step, mixed_land.at[step - 1], came, gy)
        put_output(came, mixed_land.at[step - 1])

    for t in (0, 1):
        alone = jnp.logical_and(selfish, y == t)
        for k, (mine, out) in enumerate(trio):

            @pl.when(jnp.logical_not(alone))
            def _():
                made = pltpu.make_async_remote_copy(
                    src_ref=row_pair(mine, t, out), dst_ref=out.at[t],
                    send_sem=send.at[att + 3 * t + k], recv_sem=recv.at[att + 3 * t + k],
                    device_id=(z, 2 * gx + t), device_id_type=MESH,
                )
                made.wait_send()
                made.wait_recv()

    krows, wide = aq.shape[1:]
    head = ao.shape[1]
    for a in (0, 1):

        def put_q(r):
            gqkv[r, a * wide : (a + 1) * wide] = aq[a, r].astype(f32)
            gout[shifted(r, a * head)] = ao[a, r].astype(f32)

        over_rows(krows, 2 * wide, put_q)
        gqb[a] = ab[a].astype(f32)
    for k in (0, 1):
        for step in range(1, NY):
            came = (gy + NY - step) % NY
            theirs = pl.ds(pl.multiple_of(came * unit, unit), unit)
            ref = au.at[:, theirs] if k == 0 else ad.at[theirs]
            made = pltpu.make_async_remote_copy(
                src_ref=ref, dst_ref=ref, send_sem=fsend.at[k, step], recv_sem=frecv.at[k, step],
                device_id=(gx, came), device_id_type=MESH,
            )
            made.wait_send()
            made.wait_recv()
            if k == 0:
                gup[:, theirs] = au[:, theirs].astype(f32)
            else:
                gdown[theirs] = ad[theirs].astype(f32)

    def put_grad(p, block):
        def put(r):
            there = shifted(r, rows_of(p))
            grad_tokens[there] = cot[there].astype(f32) + block[r].astype(f32)

        over_rows(sub, 2 * part, put)

    put_grad(gx, back.at[gx])
    tail = back[gx, sub : sub + 32].astype(f32)
    for step in range(1, NX):
        came = (gx + NX - step) % NX
        post.arrived(us + step, back_land.at[step - 1], came, gy)
        put_grad(came, back_land.at[step - 1])
        tail = tail + back_land[step - 1, sub : sub + 32].astype(f32)
    gains[...] = tail
    post.close()


def scatter_all(bo, ug, dq, do, qb, du, dd, ub, own, tok, cot, cols):
    bf16, f32 = jnp.bfloat16, jnp.float32
    sub, width = own.shape
    part = width // NX
    krows = dq.shape[0] // NY
    wide = dq.shape[1]
    unit = du.shape[1]
    head = do.shape[1]
    S = jax.ShapeDtypeStruct
    V = pltpu.VMEM
    vm = pl.BlockSpec(memory_space=pltpu.VMEM)
    hb = pl.BlockSpec(memory_space=pl.ANY)
    six = [(a.shape[0] // NX, a.shape[1]) for a in (dq, do, qb, du, dd, ub)]
    return pl.pallas_call(
        scatter_kernel,
        out_shape=[
            S((NX * sub, part), bf16),
            S((NX * sub, part), f32),
            S((32, part), f32),
            S((16, width), f32),
            S((krows, NY * unit), f32),
            S((NY * unit, krows), f32),
            S((krows, 2 * wide), f32),
            S((2 * head, krows), f32),
            S((2, 16, qb.shape[1]), f32),
            S((16, unit), f32),
        ],
        in_specs=[hb] * 8 + [vm] * 4,
        out_specs=[vm] * 10,
        scratch_shapes=[
            V((4, sub, width), bf16), V((4, sub, width), bf16), V((3, sub, width), bf16),
            V((4, sub + 16, width), bf16), V((4, sub + 16, width), bf16), V((3, sub + 16, width), bf16),
        ]
        + [V((2 * r, c), bf16) for r, c in six]
        + [V((2 * r, c), bf16) for r, c in six]
        + [V((r, c), bf16) for r, c in six]
        + [V((r, c), bf16) for r, c in six]
        + [
            V((krows, NY * unit), bf16), V((NY * unit, krows), bf16), V((2, krows, wide), bf16),
            V((2, krows, head), bf16), V((2, 16, qb.shape[1]), bf16),
            V((NX, sub, part), bf16), V((NX - 1, sub, part), bf16),
            V((NX, sub + 32, part), bf16), V((NX - 1, sub + 32, part), bf16),
            pltpu.SemaphoreType.DMA((64,)), pltpu.SemaphoreType.DMA((64,)),
            pltpu.SemaphoreType.DMA((2, 8)), pltpu.SemaphoreType.DMA((2, 8)),
            pltpu.SemaphoreType.DMA((48,)),
        ],
        compiler_params=pltpu.CompilerParams(
            collective_id=1, has_side_effects=True, vmem_limit_bytes=60 * 2**20
        ),
        name="scatter_all",
    )(bo, ug, dq, do, qb, du, dd, ub, own, tok, cot, cols)


def chunk_mask(sub, gx, tile, chunk, queries, keys):
    row = lax.broadcasted_iota(jnp.int32, (queries, keys), 0)
    col = lax.broadcasted_iota(jnp.int32, (queries, keys), 1)
    span = NX * sub
    query_pos = span * (2 * tile + row // sub) + sub * gx + row % sub
    return span * chunk + col <= query_pos


def load_chunk(sub, parts, chunk, low, high):
    rows = pl.ds(pl.multiple_of(chunk * sub, sub), sub)
    return jnp.concatenate([parts[p, rows, low:high] for p in range(NX)], axis=0)


def attend_tile(sub, gx, tile, q, parts, ctx, low, log):
    rows = 2 * sub
    place = pl.ds(pl.multiple_of(tile * rows, rows), rows)
    query = q[place]

    def step(chunk, carried, masked):
        top, total, summed = carried
        keys = load_chunk(sub, parts, chunk, 0, HEAD)
        values = load_chunk(sub, parts, chunk, HEAD, 2 * HEAD)
        scores = contract_last(query, keys)
        if masked:
            visible = chunk_mask(sub, gx, tile, chunk, rows, NX * sub)
            scores = jnp.where(visible, scores, -1e30)
        new_top = jnp.maximum(top, jnp.max(scores, axis=-1, keepdims=True))
        weights = jnp.exp(scores - new_top)
        if masked:
            weights = jnp.where(visible, weights, 0.0)
        shrink = jnp.exp(top - new_top)
        total = total * shrink + jnp.sum(weights, axis=-1, keepdims=True)
        summed = summed * shrink + jnp.dot(
            weights.astype(jnp.bfloat16), values, preferred_element_type=jnp.float32
        )
        return new_top, total, summed

    state = (
        jnp.full((rows, 1), -1e30, jnp.float32),
        jnp.zeros((rows, 1), jnp.float32),
        jnp.zeros((rows, HEAD), jnp.float32),
    )
    state = lax.fori_loop(0, 2 * tile, lambda c, s: step(c, s, False), state)
    state = step(2 * tile, state, True)
    state = step(2 * tile + 1, state, True)
    top, total, summed = state
    context = summed / total
    ctx[place] = context
    low[place] = context.astype(jnp.bfloat16)
    log[place] = jnp.broadcast_to(top + jnp.log(total), (rows, log.shape[1]))


def attend_kernel(q, kv, ctx, low, log, parts, send, recv, loc):
    here = Place()
    gx, gy = here.gx, here.gy
    post = Post(send, recv)
    sub = q.shape[0] // NY
    greet([(here.near, gy), (here.far, gy)])
    own = pltpu.make_async_copy(kv, parts.at[gx], loc.at[0])
    own.start()
    slot = post.take(3)
    post.go(slot, kv, parts.at[gx], here.far, gy)
    post.go(slot + 1, kv, parts.at[gx], here.near, gy)
    post.arrived(slot, parts.at[here.far], here.far, gy)
    post.go(slot + 2, parts.at[here.far], parts.at[here.far], here.near, gy)
    own.wait()
    post.arrived(slot + 1, parts.at[here.near], here.near, gy)
    post.arrived(slot + 2, parts.at[here.over], here.near, gy)

    def tile(t, carried):
        attend_tile(sub, gx, t, q, parts, ctx, low, log)
        return carried

    lax.fori_loop(0, NY // 2, tile, 0)
    post.close()


def attend(query, kv):
    rows = query.shape[0]
    S = jax.ShapeDtypeStruct
    vm = pl.BlockSpec(memory_space=pltpu.VMEM)
    return pl.pallas_call(
        attend_kernel,
        out_shape=[
            S((rows, HEAD), jnp.float32),
            S((rows, HEAD), jnp.bfloat16),
            S((rows, 128), jnp.float32),
            S((NX,) + kv.shape, jnp.bfloat16),
        ],
        in_specs=[vm] * 2,
        out_specs=[vm] * 4,
        scratch_shapes=[pltpu.SemaphoreType.DMA((8,)), pltpu.SemaphoreType.DMA((8,)), pltpu.SemaphoreType.DMA((2,))],
        compiler_params=pltpu.CompilerParams(collective_id=2, has_side_effects=True, vmem_limit_bytes=32 * 2**20),
        name="attend",
    )(query, kv)


def attend_back_tile(sub, gx, tile, q, g, ctx, log, parts, dq, acc):
    rows = 2 * sub
    place = pl.ds(pl.multiple_of(tile * rows, rows), rows)
    query = q[place]
    grad = g[place]
    log_total = log[place, 0:1]
    delta = jnp.sum(grad.astype(jnp.float32) * ctx[place], axis=-1, keepdims=True)

    def step(chunk, carried, masked):
        keys = load_chunk(sub, parts, chunk, 0, HEAD)
        values = load_chunk(sub, parts, chunk, HEAD, 2 * HEAD)
        probs = contract_last(query, keys) - log_total
        if masked:
            visible = chunk_mask(sub, gx, tile, chunk, rows, NX * sub)
            probs = jnp.where(visible, jnp.exp(jnp.where(visible, probs, 0.0)), 0.0)
        else:
            probs = jnp.exp(probs)
        grad_probs = contract_last(grad, values)
        grad_scores = (probs * (grad_probs - delta)).astype(jnp.bfloat16)
        acc[chunk, :, 0:HEAD] += contract_first(grad_scores, query)
        acc[chunk, :, HEAD : 2 * HEAD] += contract_first(probs.astype(jnp.bfloat16), grad)
        return carried + jnp.dot(grad_scores, keys, preferred_element_type=jnp.float32)

    total = jnp.zeros((rows, HEAD), jnp.float32)
    total = lax.fori_loop(0, 2 * tile, lambda c, s: step(c, s, False), total)
    total = step(2 * tile, total, True)
    total = step(2 * tile + 1, total, True)
    dq[place] = total * HEAD ** (-0.5)


def attend_back_kernel(
    q, g, ctx, log, parts, dq, dkv, acc, low, near, mine, sent, came, send, recv, loc
):
    here = Place()
    gx, gy = here.gx, here.gy
    post = Post(send, recv)
    sub = q.shape[0] // NY
    greet([(here.near, gy), (here.far, gy)])

    def clear(chunk, carried):
        acc[chunk] = jnp.zeros(acc.shape[1:], jnp.float32)
        return carried

    lax.fori_loop(0, NY, clear, 0)

    def tile(t, carried):
        attend_back_tile(sub, gx, t, q, g, ctx, log, parts, dq, acc)
        return carried

    lax.fori_loop(0, NY // 2, tile, 0)

    def flush(chunk, carried):
        for p in range(NX):
            low[pl.ds(pl.multiple_of(p * sub * NY + chunk * sub, sub), sub)] = acc[
                chunk, p * sub : (p + 1) * sub
            ].astype(jnp.bfloat16)
        return carried

    lax.fori_loop(0, NY, flush, 0)
    locs = [0]

    def load(src, dst):
        made = pltpu.make_async_copy(src, dst, loc.at[locs[0]])
        locs[0] += 1
        made.start()
        return made

    red = Reduce(post, here, load, low, near, mine, sent, came)
    red.cross()

    def put(r, value):
        dkv[r] = value

    red.total(put)
    post.close()


def attend_back(query, grad, context, log_total, parts):
    rows = query.shape[0]
    sub = rows // NY
    S, V = jax.ShapeDtypeStruct, pltpu.VMEM
    bf16 = jnp.bfloat16
    vm = pl.BlockSpec(memory_space=pltpu.VMEM)
    width = 2 * HEAD
    return pl.pallas_call(
        attend_back_kernel,
        out_shape=[S((rows, HEAD), jnp.float32), S((rows, width), jnp.float32)],
        in_specs=[vm] * 5,
        out_specs=[vm] * 2,
        scratch_shapes=[
            V((NY, NX * sub, width), jnp.float32), V((NX * rows, width), bf16),
            V((2 * rows, width), bf16), V((2 * rows, width), bf16), V((rows, width), bf16), V((rows, width), bf16),
            pltpu.SemaphoreType.DMA((8,)), pltpu.SemaphoreType.DMA((8,)), pltpu.SemaphoreType.DMA((2,)),
        ],
        compiler_params=pltpu.CompilerParams(collective_id=3, has_side_effects=True, vmem_limit_bytes=48 * 2**20),
        name="attend_back",
    )(query, grad, context, log_total, parts)


def regroup(
    tokens,
    attn_gain,
    attn_shift,
    ffn_gain,
    ffn_shift,
    qkv_weight,
    qkv_bias,
    out_weight,
    out_bias,
    up_weight,
    up_bias,
    down_weight,
    down_bias,
    cotangent,
):
    f32, bf16 = jnp.float32, jnp.bfloat16
    gx, gy = lax.axis_index("gx"), lax.axis_index("gy")
    nx, ny = NX, NY
    block_rows, part = tokens.shape
    width = nx * part
    sub = block_rows // nx
    rows = sub * ny
    unit = up_weight.shape[1] // ny
    krows = qkv_weight.shape[0]
    head_cols = 3 * HEAD

    def line(*pieces):
        flat = jnp.concatenate(pieces)
        return jnp.pad(flat, (0, part - flat.shape[0]))[None]

    small = jnp.concatenate(
        [
            line(attn_gain, attn_shift),
            line(ffn_gain, ffn_shift),
            line(up_bias, qkv_bias),
            line(out_bias, down_bias),
            jnp.zeros((12, part), bf16),
        ]
    )
    xb, cb, wq, wo, uu, dd = gather_all(
        tokens, small, cotangent, qkv_weight, out_weight, up_weight, down_weight
    )
    cot = cb.reshape(rows, width)
    qkv_full = wq.reshape(width, head_cols)
    out_full = jnp.transpose(wo, (1, 0, 2)).reshape(HEAD, width)
    up_full = jnp.transpose(uu, (1, 0, 2)).reshape(width, nx * unit)
    down_full = dd.reshape(nx * unit, width)

    lines = xb[:, sub : sub + 4].reshape(ny, 4, nx, part).astype(f32)
    gain_attn = lines[:, 0, 0, :krows].reshape(1, width)
    shift_attn = lines[:, 0, 0, krows:].reshape(1, width)
    gain_ffn = lines[:, 1, 0, :krows].reshape(1, width)
    shift_ffn = lines[:, 1, 0, krows:].reshape(1, width)
    up_shift = lax.dynamic_index_in_dim(lines[:, 2, :, :unit], gy, 0, keepdims=False).reshape(-1)
    bias_size = qkv_bias.shape[0]
    qkv_all = jnp.transpose(lines[:, 2, :, unit : unit + bias_size], (1, 0, 2)).reshape(
        ny, head_cols
    )
    qkv_shift = lax.dynamic_index_in_dim(qkv_all, gy, 0, keepdims=False)
    mine = lax.dynamic_index_in_dim(lines[:, 3], gx, 1, keepdims=False)
    size = out_bias.shape[0]
    out_cols = mine[:, :size].reshape(1, part) + mine[:, size : 2 * size].reshape(1, part)

    full_rows = xb[:, :sub].reshape(rows, width).astype(f32)
    average = jnp.mean(full_rows, axis=-1, keepdims=True)
    centred = full_rows - average
    rate = lax.rsqrt(jnp.mean(centred * centred, axis=-1, keepdims=True) + eps_norm)
    xhat = centred * rate
    normed_attn = (xhat * gain_attn + shift_attn).astype(bf16)
    normed_ffn = (xhat * gain_ffn + shift_ffn).astype(bf16)

    position = (
        block_rows * jnp.arange(ny, dtype=jnp.int32)[:, None]
        + sub * gx
        + jnp.arange(sub, dtype=jnp.int32)[None]
    ).reshape(rows)
    angles = angle_table(position)
    mixed = jnp.dot(normed_attn, qkv_full, preferred_element_type=f32) + qkv_shift
    mixed = mixed.reshape(rows, 1, 3, HEAD)
    query = (rotate(mixed[:, :, 0], angles).astype(bf16) * jnp.asarray(HEAD ** (-0.5), bf16)).reshape(
        rows, HEAD
    )
    key = rotate(mixed[:, :, 1], angles).astype(bf16).reshape(rows, HEAD)
    value = mixed[:, :, 2].astype(bf16).reshape(rows, HEAD)
    context, context_low, log_total, kv_parts = attend(query, jnp.concatenate([key, value], axis=1))

    hidden_pre = jnp.dot(normed_ffn, up_full, preferred_element_type=f32) + up_shift
    hidden, gelu_back = jax.vjp(exact_gelu, hidden_pre)
    hidden_low = hidden.astype(bf16)
    branch = jnp.dot(hidden_low, down_full, preferred_element_type=f32) + jnp.dot(
        context_low, out_full, preferred_element_type=f32
    )
    branch = branch.astype(bf16).reshape(ny, sub, width)

    grad_context = contract_last(cot, out_full).astype(bf16)
    grad_hidden = contract_last(cot, down_full)
    grad_pre = gelu_back(grad_hidden)[0].astype(bf16)
    dq, dkv = attend_back(query, grad_context, context, log_total, kv_parts)
    spun = [
        unrotate(g.reshape(rows, 1, HEAD), angles).reshape(rows, HEAD) for g in (dq, dkv[:, :HEAD])
    ]
    grad_mixed = jnp.concatenate(spun + [dkv[:, HEAD:]], axis=1).astype(bf16)

    d_up = jnp.concatenate(
        [
            contract_first(normed_ffn, grad_pre[:, p * unit : (p + 1) * unit]).astype(bf16)
            for p in range(nx)
        ]
    )
    d_down = contract_first(hidden_low, cot).astype(bf16)
    d_up_b = jnp.sum(grad_pre.astype(f32), axis=0).astype(bf16).reshape(nx, 1, unit)
    ub = jnp.pad(d_up_b, ((0, 0), (0, 15), (0, 0))).reshape(nx * 16, unit)
    d_qkv = contract_first(normed_attn, grad_mixed).astype(bf16)
    d_out = contract_first(context_low, cot).astype(bf16)
    d_out = jnp.transpose(d_out.reshape(HEAD, ny, krows), (1, 0, 2)).reshape(ny * HEAD, krows)
    d_qkv_b = jnp.sum(grad_mixed.astype(f32), axis=0).astype(bf16).reshape(4, 1, bias_size)
    qb = jnp.pad(
        jnp.concatenate([d_qkv_b, d_qkv_b]), ((0, 0), (0, 15), (0, krows - bias_size))
    ).reshape(ny * 16, krows)

    grad_norm_attn = contract_last(grad_mixed, qkv_full)
    grad_norm_ffn = contract_last(grad_pre, up_full)
    u = (grad_norm_attn * gain_attn + grad_norm_ffn * gain_ffn).astype(bf16)
    sums = jnp.stack(
        [
            jnp.sum(grad_norm_attn * xhat, axis=0),
            jnp.sum(grad_norm_attn, axis=0),
            jnp.sum(grad_norm_ffn * xhat, axis=0),
            jnp.sum(grad_norm_ffn, axis=0),
        ]
    ).reshape(4, ny, krows)
    cot_sum = jnp.sum(cotangent.astype(f32), axis=0).reshape(1, ny, size)
    cot_sum = jnp.pad(cot_sum, ((0, 0), (0, 0), (0, krows - size)))
    rest = jnp.concatenate([sums, cot_sum, jnp.zeros((3, ny, krows), f32)])
    rest = jnp.transpose(rest, (1, 0, 2)).reshape(ny, 1, width).astype(bf16)
    ug = jnp.concatenate(
        [u.reshape(ny, sub, width), jnp.pad(rest, ((0, 0), (0, 15), (0, 0)))], axis=1
    )
    own = lax.dynamic_index_in_dim(xb, gy, 0, keepdims=False)[:sub]
    output, grad_tokens, gains, smalls, gup, gdown, gqkv, gout, gqb, gub = scatter_all(
        branch, ug, d_qkv, d_out, qb, d_up, d_down, ub, own, tokens, cotangent, out_cols
    )
    gain_sum = gains.reshape(2, 16, part)[:, 0].reshape(4, krows)
    grad_bias = smalls[0, 4 * krows : 4 * krows + size]
    grad_qkv_b = jnp.where(gy < 4, gqb[0, 0], gqb[1, 0])[:bias_size]
    return (
        output,
        grad_tokens,
        gain_sum[0],
        gain_sum[1],
        gain_sum[2],
        gain_sum[3],
        gqkv,
        grad_qkv_b,
        gout,
        grad_bias,
        gup,
        gub[0],
        gdown,
        grad_bias,
    )


def solution(mesh):
    placed = (
        P("gy", "gx"),
        P("gy"),
        P("gy"),
        P("gy"),
        P("gy"),
        P("gy", "gx"),
        P(("gx", "gy")),
        P("gx", "gy"),
        P(("gx", "gy")),
        P("gy", "gx"),
        P(("gx", "gy")),
        P("gx", "gy"),
        P(("gx", "gy")),
        P("gy", "gx"),
    )
    return jax.shard_map(
        regroup if mesh.shape["gy"] == NY == SPAN and mesh.shape["gx"] == NX else local,
        mesh=mesh,
        in_specs=placed,
        out_specs=(
            P("gy", "gx"),
            P("gy", "gx"),
            P("gy"),
            P("gy"),
            P("gy"),
            P("gy"),
            P("gy", "gx"),
            P(("gx", "gy")),
            P("gx", "gy"),
            P(("gx", "gy")),
            P("gy", "gx"),
            P(("gx", "gy")),
            P("gx", "gy"),
            P(("gx", "gy")),
        ),
        check_vma=False,
    )
```
